256 devices in a mesh: leaf: 32 (over x, z), row: 8 (over y, core).
Axes of the slice: x: 4, y: 4, z: 8, core: 2. Of those that a mesh axis runs over, the one named last changes fastest.
Arguments:
- leaf_probes: bfloat16 [32, 2048, 128], P('leaf', 'row'), may hold values from -6 to 6
- lower_probes: bfloat16 [4, 4096, 128], P(None, ('leaf', 'row')), may hold values from -6 to 6
- middle_probes: bfloat16 [2, 8192, 128], P(None, ('leaf', 'row')), may hold values from -6 to 6
- root_probes: bfloat16 [16384, 128], P(('leaf', 'row')), may hold values from -6 to 6
- leaf_inverse: bfloat16 [32, 2048, 2048], P('leaf', 'row'), as said below
- lower_inverse: bfloat16 [4, 4096, 4096], P(None, 'row', 'leaf'), as said below
- middle_inverse: bfloat16 [2, 8192, 8192], P(None, 'row', 'leaf'), as said below
- root_inverse: bfloat16 [16384, 16384], P('row', 'leaf'), as said below
- leaf_panel: bfloat16 [32, 512, 2048], P('leaf', 'row'), may hold values from -0.09375 to 0.09375
- lower_to_middle: bfloat16 [4, 8192, 4096], P(None, 'leaf', 'row'), may hold values from -0.125 to 0.125
- lower_to_root: bfloat16 [4, 16384, 4096], P(None, 'leaf', 'row'), may hold values from -0.125 to 0.125
- middle_to_root: bfloat16 [2, 16384, 8192], P(None, 'leaf', 'row'), may hold values from -0.09375 to 0.09375
- leaf_parent: int32 [32], replicated, may hold values from 0 to 3
- leaf_blocks: int32 [32, 4], replicated, may hold values from 0 to 127, as said below
Outputs:
- leaf_solution: bfloat16 [32, 2048, 128], P('leaf', 'row')
- lower_solution: bfloat16 [4, 4096, 128], P(None, ('leaf', 'row'))
- middle_solution: bfloat16 [2, 8192, 128], P(None, ('leaf', 'row'))
- root_solution: bfloat16 [16384, 128], P(('leaf', 'row'))
The draws below stay inside these ranges and needn't reach their ends.
Inputs may be any that keep to these rules, and one draw needn't show every extreme that they name: `leaf_inverse`: every inverse of a diagonal factor block is lower triangular: entries above its diagonal are zero. `lower_inverse`: every inverse of a diagonal factor block is lower triangular: entries above its diagonal are zero. `middle_inverse`: every inverse of a diagonal factor block is lower triangular: entries above its diagonal are zero. `root_inverse`: every inverse of a diagonal factor block is lower triangular: entries above its diagonal are zero. `leaf_blocks`: columns 0 and 1 are two different blocks of 128 rows of the parent separator, column 2 a block of the second-level separator above it, column 3 a block of the root.
All inputs are finite; a program needn't handle non-finite values.
Results may differ from the reference program's by a relative error of at most 0.04.
Values may be sent and summed in bfloat16 or wider, within the bound.
No kernel may reach another device: no remote copies, remote signals or barrier semaphores. Data moves between devices by JAX's collectives and lax.ppermute only.
A program may use at most 64 MiB of HBM per device.

```python
import math
import jax
import jax.numpy as jnp
import numpy as np
from jax import lax

PROBES = 128
LEAF_ORDER = 2048
LOWER_ORDER = 4096
MIDDLE_ORDER = 8192
ROOT_ORDER = 16384
BLOCK = 128
PANEL = 512
LEAVES = 32


def triangle_draw(key, members, matrix_order):
    key_below, key_middle = jax.random.split(key)
    full_shape = (members, matrix_order, matrix_order)
    values = jax.random.normal(key_below, full_shape, jnp.float32)
    leading = jax.random.uniform(key_middle, (members, matrix_order, 1), jnp.float32, 0.6, 1.4)
    row_ids = lax.broadcasted_iota(jnp.int32, (1, matrix_order, 1), 1)
    column_ids = lax.broadcasted_iota(jnp.int32, (1, 1, matrix_order), 2)
    below = jnp.where(column_ids < row_ids, values * (0.6 / math.sqrt(matrix_order)), 0.0)
    return below + jnp.where(column_ids == row_ids, leading, 0.0)


def draw_leaf_inverse(key, part):
    return triangle_draw(key, LEAVES, LEAF_ORDER).astype(jnp.bfloat16)


def draw_lower_inverse(key, part):
    return triangle_draw(key, 4, LOWER_ORDER).astype(jnp.bfloat16)


def draw_middle_inverse(key, part):
    return triangle_draw(key, 2, MIDDLE_ORDER).astype(jnp.bfloat16)


def draw_root_inverse(key, part):
    return triangle_draw(key, 1, ROOT_ORDER)[0].astype(jnp.bfloat16)


def draw_leaf_blocks(key, part):
    key_list = jax.random.split(key, 4)
    lower_count = LOWER_ORDER // BLOCK
    first_block = jax.random.randint(key_list[0], (LEAVES, 1), 0, lower_count)
    second_block = (first_block + jax.random.randint(key_list[1], (LEAVES, 1), 1, lower_count)) % lower_count
    middle_block = jax.random.randint(key_list[2], (LEAVES, 1), 0, MIDDLE_ORDER // BLOCK)
    middle_block = middle_block.at[0, 0].set(0)
    root_block = jax.random.randint(key_list[3], (LEAVES, 1), 0, ROOT_ORDER // BLOCK)
    root_block = root_block.at[0, 0].set(ROOT_ORDER // BLOCK - 1)
    return jnp.concatenate([first_block, second_block, middle_block, root_block], axis=1).astype(jnp.int32)


def place_ends(entries, own_key, low, top_value):
    longest = entries.shape.index(max(entries.shape))
    spots = []
    for shift in (0, 1):
        where = [jax.random.randint(jax.random.fold_in(own_key, axis), (), 0, length) for axis, length in enumerate(entries.shape)]
        where[longest] = (where[longest] + shift) % entries.shape[longest]
        spots.append(tuple(where))
    return entries.at[spots[0]].set(low).at[spots[1]].set(top_value)


def with_spikes(drawn, stream_key, source, target, parts, factor):
    def block_of(position):
        return (jnp.arange(drawn.shape[position]) // (drawn.shape[position] // parts)).reshape((-1,) + (1,) * (drawn.ndim - 1 - position))

    first = jax.random.permutation(stream_key, parts)[block_of(target)]
    other_side = (block_of(target) + parts // 2) % parts
    return jnp.where((block_of(source) == first) | (block_of(source) == other_side), factor * drawn, drawn)


def block_scale(stream_key, dims, cuts, least, high):
    gain, own = 1.0, jax.random.fold_in(stream_key, 6)
    for axis_at, blocks in cuts:
        draws = jnp.exp(jax.random.uniform(jax.random.fold_in(own, axis_at), (blocks,), jnp.float32, least / len(cuts), high / len(cuts)))
        gain = gain * jnp.repeat(draws, dims[axis_at] // blocks).reshape([-1 if axis == axis_at else 1 for axis in range(len(dims))])
    return gain


def rank_table(amount, slope):
    loads = [(1 << 20) // math.isqrt(grade ** slope) + 1 for grade in range(1, amount + 1)]
    width = 1 + sum(loads) // (1 << 30)
    return np.cumsum(np.array([max(1, weight // width) for weight in loads]))


def skewed_ids(rng, dims, amount, skew):
    table = rank_table(amount, skew)
    lot = jax.random.randint(jax.random.fold_in(rng, 1), dims, 0, int(table[amount - 1]))
    grade = jnp.searchsorted(jnp.asarray(table, jnp.int32), lot, side="right")
    return jax.random.permutation(jax.random.fold_in(rng, 2), amount)[grade].astype(jnp.int32)


def scatter_about(rng, extent, width, reach, shards=(), held_as=jnp.bfloat16):
    entries = width * jax.random.normal(rng, extent, jnp.float32)
    if shards:
        entries = entries * block_scale(rng, extent, shards, -0.22, 0.18)
    return jnp.clip(entries, -reach, reach).astype(held_as)


def heavy_noise(key, dims, scale, limit, pieces, heavy, kind=jnp.bfloat16):
    values = scale * jax.random.normal(key, dims, jnp.float32)
    if pieces:
        values = values * block_scale(key, dims, pieces, -0.22, 0.18)
    return jnp.clip(with_spikes(values, jax.random.fold_in(key, 3), *heavy), -limit, limit).astype(kind)


def setup_inputs(seed: int = 0) -> dict:
    seeds = jax.random.split(jax.random.key(seed), 15)
    leaf_probes = scatter_about(seeds[0], (LEAVES, LEAF_ORDER, PROBES), 1.0, 6.0, ((0, 32), (1, 8)))
    lower_probes = scatter_about(seeds[1], (4, LOWER_ORDER, PROBES), 1.0, 6.0, ((1, 256),))
    middle_probes = scatter_about(seeds[2], (2, MIDDLE_ORDER, PROBES), 1.0, 6.0, ((1, 256),))
    root_probes = scatter_about(seeds[3], (ROOT_ORDER, PROBES), 1.0, 6.0, ((0, 256),))
    leaf_inverse = draw_leaf_inverse(jax.random.fold_in(seeds[14], 71), 0)
    lower_inverse = draw_lower_inverse(jax.random.fold_in(seeds[14], 71), 0)
    middle_inverse = draw_middle_inverse(jax.random.fold_in(seeds[14], 71), 0)
    root_inverse = draw_root_inverse(jax.random.fold_in(seeds[14], 71), 0)
    leaf_panel = scatter_about(seeds[8], (LEAVES, PANEL, LEAF_ORDER), (2 * LEAF_ORDER) ** -0.5, 0.09375, ((0, 32), (1, 8)))
    lower_to_middle = heavy_noise(seeds[9], (4, MIDDLE_ORDER, LOWER_ORDER), (2 * LOWER_ORDER) ** -0.5, 0.125, ((1, 32), (2, 8)), (1, 2, 32, 2.75))
    lower_to_root = heavy_noise(seeds[10], (4, ROOT_ORDER, LOWER_ORDER), (2 * LOWER_ORDER) ** -0.5, 0.125, ((1, 32), (2, 8)), (1, 2, 32, 2.75))
    middle_to_root = heavy_noise(seeds[11], (2, ROOT_ORDER, MIDDLE_ORDER), (2 * MIDDLE_ORDER) ** -0.5, 0.09375, ((1, 32), (2, 8)), (1, 2, 32, 2.75))
    leaf_parent = place_ends(skewed_ids(seeds[12], (LEAVES,), 4, 2), jax.random.fold_in(seeds[12], 3), 0, 3).astype(jnp.int32)
    leaf_blocks = draw_leaf_blocks(jax.random.fold_in(seeds[14], 71), 0)
    return {"leaf_probes": leaf_probes, "lower_probes": lower_probes, "middle_probes": middle_probes, "root_probes": root_probes, "leaf_inverse": leaf_inverse, "lower_inverse": lower_inverse, "middle_inverse": middle_inverse, "root_inverse": root_inverse, "leaf_panel": leaf_panel, "lower_to_middle": lower_to_middle, "lower_to_root": lower_to_root, "middle_to_root": middle_to_root, "leaf_parent": leaf_parent, "leaf_blocks": leaf_blocks}


def product(left, right):
    return jnp.dot(left, right, preferred_element_type=jnp.float32)


def rounded(values):
    return lax.optimization_barrier(values.astype(jnp.bfloat16)).astype(jnp.float32)


def target_rows(leaf_parent, leaf_blocks):
    offsets = jnp.arange(BLOCK, dtype=jnp.int32)[None, :]
    parent_base = leaf_parent * LOWER_ORDER
    first_rows = (parent_base + leaf_blocks[:, 0] * BLOCK)[:, None] + offsets
    second_rows = (parent_base + leaf_blocks[:, 1] * BLOCK)[:, None] + offsets
    middle_rows = ((leaf_parent // 2) * MIDDLE_ORDER + leaf_blocks[:, 2] * BLOCK)[:, None] + offsets
    root_rows = (leaf_blocks[:, 3] * BLOCK)[:, None] + offsets
    return first_rows, second_rows, middle_rows, root_rows


def reference(leaf_probes, lower_probes, middle_probes, root_probes, leaf_inverse, lower_inverse, middle_inverse, root_inverse, leaf_panel, lower_to_middle, lower_to_root, middle_to_root, leaf_parent, leaf_blocks):
    probe_count = leaf_probes.shape[-1]
    leaf_solved = jnp.einsum("lab,lbp->lap", leaf_inverse.astype(jnp.float32), leaf_probes.astype(jnp.float32)).astype(jnp.bfloat16)
    leaf_update = rounded(jnp.einsum("lkb,lbp->lkp", leaf_panel.astype(jnp.float32), leaf_solved.astype(jnp.float32)))
    first_rows, second_rows, middle_rows, root_rows = target_rows(leaf_parent, leaf_blocks)

    def panel_block(number):
        return leaf_update[:, number * BLOCK:(number + 1) * BLOCK].reshape(-1, probe_count)

    lower_added = jnp.zeros((4 * LOWER_ORDER, probe_count), jnp.float32)
    lower_added = lower_added.at[first_rows.reshape(-1)].add(panel_block(0))
    lower_added = lower_added.at[second_rows.reshape(-1)].add(panel_block(1))
    middle_added = jnp.zeros((2 * MIDDLE_ORDER, probe_count), jnp.float32).at[middle_rows.reshape(-1)].add(panel_block(2))
    root_added = jnp.zeros((ROOT_ORDER, probe_count), jnp.float32).at[root_rows.reshape(-1)].add(panel_block(3))

    lower_input = (lower_probes.astype(jnp.float32) - lower_added.reshape(4, LOWER_ORDER, probe_count)).astype(jnp.bfloat16)
    lower_solved = jnp.stack([product(lower_inverse[member], lower_input[member]) for member in range(4)]).astype(jnp.bfloat16)
    lower_terms = [product(lower_to_middle[member], lower_solved[member]) for member in range(4)]
    middle_total = middle_added.reshape(2, MIDDLE_ORDER, probe_count) + jnp.stack([lower_terms[0] + lower_terms[1], lower_terms[2] + lower_terms[3]])
    middle_input = (middle_probes.astype(jnp.float32) - middle_total).astype(jnp.bfloat16)
    middle_solved = jnp.stack([product(middle_inverse[member], middle_input[member]) for member in range(2)]).astype(jnp.bfloat16)
    root_total = root_added
    for member in range(4):
        root_total = root_total + product(lower_to_root[member], lower_solved[member])
    for member in range(2):
        root_total = root_total + product(middle_to_root[member], middle_solved[member])
    root_input = (root_probes.astype(jnp.float32) - root_total).astype(jnp.bfloat16)
    root_solved = product(root_inverse, root_input).astype(jnp.bfloat16)

    root_solution = product(root_inverse.T, root_solved).astype(jnp.bfloat16)
    middle_reduced = jnp.stack([middle_solved[member].astype(jnp.float32) - product(middle_to_root[member].T, root_solution) for member in range(2)]).astype(jnp.bfloat16)
    middle_solution = jnp.stack([product(middle_inverse[member].T, middle_reduced[member]) for member in range(2)]).astype(jnp.bfloat16)
    lower_reduced = jnp.stack([lower_solved[member].astype(jnp.float32) - product(lower_to_middle[member].T, middle_solution[member // 2]) - product(lower_to_root[member].T, root_solution) for member in range(4)]).astype(jnp.bfloat16)
    lower_solution = jnp.stack([product(lower_inverse[member].T, lower_reduced[member]) for member in range(4)]).astype(jnp.bfloat16)

    lower_flat = lower_solution.reshape(-1, probe_count)
    middle_flat = middle_solution.reshape(-1, probe_count)
    ancestor = jnp.concatenate([lower_flat[first_rows], lower_flat[second_rows], middle_flat[middle_rows], root_solution[root_rows]], axis=1)
    leaf_back = jnp.einsum("lkb,lkp->lbp", leaf_panel.astype(jnp.float32), ancestor.astype(jnp.float32))
    leaf_reduced = (leaf_solved.astype(jnp.float32) - leaf_back).astype(jnp.bfloat16)
    leaf_solution = jnp.einsum("lab,lap->lbp", leaf_inverse.astype(jnp.float32), leaf_reduced.astype(jnp.float32)).astype(jnp.bfloat16)
    return leaf_solution, lower_solution, middle_solution, root_solution
```

```python
import jax
import jax.numpy as jnp
from jax import lax
from jax.sharding import Mesh, PartitionSpec as P

LEAF = ("x", "z")
ROW = ("y", "core")
LEAVES = 32
ROWS = 8
HALF = 64
F32 = jnp.float32
BF16 = jnp.bfloat16


def swap(pieces, axes):
    return lax.all_to_all(pieces, axes, split_axis=0, concat_axis=0, tiled=True)


def leaf_scatter(partial):
    pieces = partial.astype(BF16).reshape(LEAVES, HALF, -1)
    return jnp.sum(swap(pieces, LEAF).astype(F32), axis=0)


def leaf_gather(piece):
    pieces = swap(jnp.broadcast_to(piece[None], (LEAVES,) + piece.shape), LEAF)
    return pieces.reshape((-1,) + piece.shape[1:])


def row_scatter(partial):
    pieces = partial.astype(BF16).reshape(ROWS, -1, partial.shape[-1])
    return jnp.sum(swap(pieces, ROW).astype(F32), axis=0)


def row_gather(piece):
    return lax.all_gather(piece, ROW, axis=0, tiled=False)


def core_swap(half):
    return lax.ppermute(half, "core", [(0, 1), (1, 0)])


def both_halves(half, core):
    other = core_swap(half)
    first = jnp.where(core == 0, half, other)
    second = jnp.where(core == 0, other, half)
    return jnp.stack([first, second])


def row_half_sum(partial, core):
    rounded = partial.astype(BF16)
    mine = jnp.where(core == 0, partial[0], partial[1])
    theirs = jnp.where(core == 0, rounded[1], rounded[0])
    pair = (mine + core_swap(theirs).astype(F32)).astype(BF16)
    gathered = swap(jnp.broadcast_to(pair[None], (4,) + pair.shape), "y")
    return jnp.sum(gathered.astype(F32), axis=0)


def dot(spec, left, right):
    return jnp.einsum(spec, left, right, preferred_element_type=F32)


def body(
    leaf_probes,
    lower_probes,
    middle_probes,
    root_probes,
    leaf_inverse,
    lower_inverse,
    middle_inverse,
    root_inverse,
    leaf_panel,
    lower_to_middle,
    lower_to_root,
    middle_to_root,
    leaf_parent,
    leaf_blocks,
):
    leaf = lax.axis_index("x") * 8 + lax.axis_index("z")
    y = lax.axis_index("y")
    core = lax.axis_index("core")
    row = y * 2 + core
    probes = leaf_probes.shape[-1]
    inverse = leaf_inverse[0]
    panel = leaf_panel[0]

    block = lax.dynamic_index_in_dim(leaf_blocks, y, axis=1, keepdims=False)
    parent = leaf_parent
    slot = jnp.where(
        y < 2,
        jnp.where(block == leaf, parent, -1),
        jnp.where(
            y == 2,
            jnp.where(block // 2 == leaf, (parent // 2) * 2 + block % 2, -1),
            jnp.where(block // 4 == leaf, block % 4, -1),
        ),
    )
    chosen = (slot[None, :] == jnp.arange(4, dtype=jnp.int32)[:, None]).astype(F32)

    own = jnp.concatenate(
        [
            leaf_probes[0],
            lower_probes.reshape(-1, probes),
            middle_probes.reshape(-1, probes),
            root_probes,
        ]
    )
    held = row_gather(own)
    leaf_columns = held[:, :256].reshape(-1, probes)
    lower_own = held[:, 256:320].reshape(8, 4, 16, probes).transpose(1, 0, 2, 3).reshape(4, 2, HALF, probes)
    middle_own = held[:, 320:384].reshape(8, 2, 32, probes).transpose(1, 0, 2, 3).reshape(2, 256, probes)
    root_own = held[:, 384:].reshape(2, 256, probes)

    leaf_solved = dot("ab,bp->ap", inverse, leaf_columns).astype(BF16)
    leaf_whole = row_gather(leaf_solved).reshape(-1, probes)
    leaf_update = dot("kb,bp->kp", panel, leaf_whole).astype(BF16)
    received = swap(jnp.broadcast_to(leaf_update[None], (LEAVES, HALF, probes)), LEAF).astype(F32)
    landed = jnp.sum(chosen[:, :, None, None] * received[None], axis=1).astype(BF16)
    by_level = swap(jnp.broadcast_to(landed[None], (4,) + landed.shape), "y")
    lower_added = by_level[0].astype(F32) + by_level[1].astype(F32)
    lower_half = lax.dynamic_index_in_dim(lower_own, core, axis=1, keepdims=False)
    lower_half = (lower_half.astype(F32) - lower_added).astype(BF16)
    lower_input = both_halves(lower_half, core).transpose(1, 0, 2, 3).reshape(4, 128, probes)
    upper_added = both_halves(by_level[2:], core)
    middle_added = upper_added[:, 0].reshape(2, 2, 2, HALF, probes).transpose(1, 2, 0, 3, 4).reshape(2, 256, probes)
    root_added = upper_added[:, 1].transpose(1, 0, 2, 3).reshape(2, 256, probes)
    middle_base = middle_own.astype(F32) - middle_added.astype(F32)
    root_base = root_own.astype(F32) - root_added.astype(F32)

    lower_solved = leaf_scatter(dot("smn,snp->smp", lower_inverse, lower_input)).astype(BF16)
    lower_block = leaf_gather(lower_solved).reshape(4, 512, probes)
    to_middle = dot("san,snp->sap", lower_to_middle, lower_block)
    to_middle = to_middle.reshape(2, 2, 256, probes).sum(axis=1)
    middle_sum = row_half_sum(to_middle, core)
    middle_half = (lax.dynamic_index_in_dim(middle_base, core, axis=0, keepdims=False) - middle_sum).astype(BF16)
    middle_input = both_halves(middle_half, core)
    to_root = dot("san,snp->sap", lower_to_root, lower_block).sum(axis=0)

    middle_solved = leaf_scatter(dot("smn,snp->smp", middle_inverse, middle_input)).astype(BF16)
    middle_block = leaf_gather(middle_solved).reshape(2, 1024, probes)
    to_root = to_root + dot("san,snp->sap", middle_to_root, middle_block).sum(axis=0)
    root_sum = row_half_sum(to_root.reshape(2, 256, probes), core)
    root_half = (lax.dynamic_index_in_dim(root_base, core, axis=0, keepdims=False) - root_sum).astype(BF16)
    root_input = both_halves(root_half, core).reshape(512, probes)

    root_solved = leaf_scatter(dot("mn,np->mp", root_inverse, root_input)).astype(BF16)
    root_rows = leaf_gather(root_solved)
    root_half = row_half_sum(dot("mn,mp->np", root_inverse, root_rows).reshape(2, 256, probes), core).astype(BF16)
    root_columns = both_halves(root_half, core).reshape(512, probes)

    middle_drop = leaf_scatter(dot("san,ap->snp", middle_to_root, root_columns))
    middle_reduced = (middle_solved.astype(F32) - middle_drop).astype(BF16)
    middle_rows = leaf_gather(middle_reduced).reshape(2, 1024, probes)
    middle_half = row_half_sum(dot("smn,smp->snp", middle_inverse, middle_rows), core).astype(BF16)
    middle_columns = both_halves(middle_half, core)

    lower_drop = dot("san,ap->snp", lower_to_root, root_columns)
    lower_drop = lower_drop + dot(
        "qsan,qap->qsnp", lower_to_middle.reshape(2, 2, 256, 512), middle_columns
    ).reshape(4, 512, probes)
    lower_reduced = (lower_solved.astype(F32) - leaf_scatter(lower_drop)).astype(BF16)
    lower_rows = leaf_gather(lower_reduced).reshape(4, 512, probes)
    lower_half = row_half_sum(dot("smn,smp->snp", lower_inverse, lower_rows).reshape(2, 256, probes), core)
    lower_columns = both_halves(lower_half.astype(BF16), core).reshape(4, 128, probes)

    stacked = jnp.where(
        y < 2,
        lower_columns.reshape(4, 2, HALF, probes),
        jnp.where(
            y == 2,
            middle_columns.reshape(4, 2, HALF, probes),
            root_columns.reshape(4, 2, HALF, probes),
        ),
    )
    table = lax.dynamic_index_in_dim(stacked, core, axis=1, keepdims=False)
    sent = jnp.sum(chosen[:, :, None, None] * table[:, None].astype(F32), axis=0).astype(BF16)
    ancestor = jnp.sum(swap(sent, LEAF).astype(F32), axis=0).astype(BF16)
    leaf_back = row_scatter(dot("kb,kp->bp", panel, ancestor))
    leaf_reduced = (leaf_solved.astype(F32) - leaf_back).astype(BF16)
    leaf_solution = row_scatter(dot("ab,ap->bp", inverse, leaf_reduced)).astype(BF16)

    lower_solution = lax.dynamic_slice_in_dim(lower_columns, row * 16, 16, axis=1)
    middle_solution = lax.dynamic_slice_in_dim(middle_columns, row * 32, 32, axis=1)
    root_solution = lax.dynamic_slice_in_dim(root_columns, row * 64, 64, axis=0)
    return (leaf_solution[None], lower_solution, middle_solution, root_solution)


def solution(mesh):
    fine = Mesh(mesh.devices.reshape(4, 8, 4, 2), ("x", "z", "y", "core"))
    every = LEAF + ROW
    return jax.shard_map(
        body,
        mesh=fine,
        in_specs=(
            P(LEAF, ROW, None),
            P(None, every, None),
            P(None, every, None),
            P(every, None),
            P(LEAF, ROW, None),
            P(None, ROW, LEAF),
            P(None, ROW, LEAF),
            P(ROW, LEAF),
            P(LEAF, ROW, None),
            P(None, LEAF, ROW),
            P(None, LEAF, ROW),
            P(None, LEAF, ROW),
            P(),
            P(),
        ),
        out_specs=(
            P(LEAF, ROW, None),
            P(None, every, None),
            P(None, every, None),
            P(every, None),
        ),
        check_vma=False,
    )
```

```python
import jax
import jax.numpy as jnp
from jax import lax
from jax.sharding import Mesh, PartitionSpec as P

LEAF = ("x", "z")
ROW = ("y", "core")
LEAVES = 32
ROWS = 8
HALF = 64
F32 = jnp.float32
BF16 = jnp.bfloat16


def swap(pieces, axes):
    return lax.all_to_all(pieces, axes, split_axis=0, concat_axis=0, tiled=True)


def total(pieces):
    return jnp.sum(pieces.astype(F32), axis=0)


def copies(piece, count):
    return jnp.broadcast_to(piece[None], (count,) + piece.shape)


def leaf_scatter(partial):
    return total(swap(partial.astype(BF16).reshape(LEAVES, HALF, -1), LEAF))


def leaf_gather(piece):
    return swap(copies(piece, LEAVES), LEAF).reshape((-1,) + piece.shape[1:])


def z_scatter(partial):
    return total(swap(partial.astype(BF16).reshape(8, HALF, -1), "z"))


def z_gather(piece):
    return swap(copies(piece, 8), "z").reshape((-1,) + piece.shape[1:])


def shift(piece, axis, step):
    return lax.ppermute(piece, axis, [(i, (i + step) % 4) for i in range(4)])


def core_swap(half):
    return lax.ppermute(half, "core", [(0, 1), (1, 0)])


def both_halves(half, core):
    other = core_swap(half)
    first = jnp.where(core == 0, half, other)
    second = jnp.where(core == 0, other, half)
    return jnp.stack([first, second])


def row_gather(piece, core):
    mine = swap(copies(piece, 4), "y")
    other = core_swap(mine)
    first = jnp.where(core == 0, mine, other)
    second = jnp.where(core == 0, other, mine)
    return jnp.stack([first, second], axis=1)


def pair_sum(halves, core):
    mine = jnp.where(core == 0, halves[0], halves[1])
    theirs = jnp.where(core == 0, halves[1], halves[0])
    return (mine.astype(F32) + core_swap(theirs).astype(F32)).astype(BF16)


def row_half_sum(partial, core):
    pair = pair_sum(partial.astype(BF16), core)
    others = [shift(pair, "y", step) for step in (1, 2, 3)]
    return sum([piece.astype(F32) for piece in others], pair.astype(F32))


def row_scatter(partial, core):
    halves = partial.astype(BF16).reshape(4, 2, 256, -1).transpose(1, 0, 2, 3)
    return total(swap(pair_sum(halves, core), "y"))


def dot(spec, left, right):
    return jnp.einsum(spec, left, right, preferred_element_type=F32)


def body(
    leaf_probes,
    lower_probes,
    middle_probes,
    root_probes,
    leaf_inverse,
    lower_inverse,
    middle_inverse,
    root_inverse,
    leaf_panel,
    lower_to_middle,
    lower_to_root,
    middle_to_root,
    leaf_parent,
    leaf_blocks,
):
    x = lax.axis_index("x")
    z = lax.axis_index("z")
    leaf = x * 8 + z
    y = lax.axis_index("y")
    core = lax.axis_index("core")
    row = y * 2 + core
    probes = leaf_probes.shape[-1]
    inverse = leaf_inverse[0]
    panel = leaf_panel[0]

    lower_held = jnp.concatenate([lower_inverse, lower_probes], axis=1)
    lower_tiles = [lax.dynamic_index_in_dim(lower_held, x, axis=0, keepdims=False)]
    for step in (1, 2, 3):
        leaving = lax.dynamic_index_in_dim(lower_held, (x + step) % 4, axis=0, keepdims=False)
        lower_tiles.append(shift(leaving, "x", step))
    lower_square = jnp.concatenate([tile[:512] for tile in lower_tiles], axis=1)
    lower_pieces = jnp.concatenate([tile[512:] for tile in lower_tiles])

    block = lax.dynamic_index_in_dim(leaf_blocks, y, axis=1, keepdims=False)
    parent = leaf_parent
    slot = jnp.where(
        y < 2,
        jnp.where((parent == x) & (block % 8 == z), (x + 4 - block // 8) % 4, -1),
        jnp.where(
            y == 2,
            jnp.where(block // 2 == leaf, (parent // 2) * 2 + block % 2, -1),
            jnp.where(block // 4 == leaf, block % 4, -1),
        ),
    )
    chosen = (slot[None, :] == jnp.arange(4, dtype=jnp.int32)[:, None]).astype(F32)

    first_held = row_gather(
        jnp.concatenate([leaf_probes[0], middle_probes.reshape(-1, probes), root_probes]), core
    ).reshape(8, 384, probes)
    leaf_columns = first_held[:, :256].reshape(-1, probes)
    middle_own = first_held[:, 256:320].reshape(8, 2, 32, probes).transpose(1, 0, 2, 3).reshape(2, 256, probes)
    root_own = first_held[:, 320:].reshape(2, 256, probes)
    leaf_solved = dot("ab,bp->ap", inverse, leaf_columns).astype(BF16)
    second_held = row_gather(jnp.concatenate([leaf_solved, lower_pieces]), core).reshape(8, 320, probes)
    leaf_whole = second_held[:, :256].reshape(-1, probes)
    lower_own = second_held[:, 256:].reshape(8, 4, 16, probes).transpose(1, 0, 2, 3).reshape(4, 2, HALF, probes)
    leaf_update = dot("kb,bp->kp", panel, leaf_whole).astype(BF16)
    received = swap(copies(leaf_update, LEAVES), LEAF).astype(F32)
    landed = jnp.sum(chosen[:, :, None, None] * received[None], axis=1).astype(BF16)
    by_step = [landed] + [shift(landed, "y", step) for step in (1, 2, 3)]

    def added_at(levels):
        parts = [
            jnp.where(levels((y + 4 - step) % 4), piece.astype(F32), 0.0) for step, piece in enumerate(by_step)
        ]
        return sum(parts[1:], parts[0])

    lower_half = lax.dynamic_index_in_dim(lower_own, core, axis=1, keepdims=False)
    lower_half = (lower_half.astype(F32) - added_at(lambda b: b < 2)).astype(BF16)
    lower_input = both_halves(lower_half, core).transpose(1, 0, 2, 3).reshape(512, probes)
    upper_half = jnp.stack([added_at(lambda b: b == 2), added_at(lambda b: b == 3)]).astype(BF16)
    upper_added = both_halves(upper_half, core)
    middle_added = upper_added[:, 0].reshape(2, 2, 2, HALF, probes).transpose(1, 2, 0, 3, 4).reshape(2, 256, probes)
    root_added = upper_added[:, 1].transpose(1, 0, 2, 3).reshape(2, 256, probes)
    middle_base = middle_own.astype(F32) - middle_added.astype(F32)
    root_base = root_own.astype(F32) - root_added.astype(F32)

    lower_solved = z_scatter(dot("mn,np->mp", lower_square, lower_input)).astype(BF16)
    lower_block = leaf_gather(lower_solved).reshape(4, 512, probes)
    to_middle = dot("san,snp->sap", lower_to_middle, lower_block)
    to_middle = to_middle.reshape(2, 2, 256, probes).sum(axis=1)
    middle_sum = row_half_sum(to_middle, core)
    middle_half = (lax.dynamic_index_in_dim(middle_base, core, axis=0, keepdims=False) - middle_sum).astype(BF16)
    middle_input = both_halves(middle_half, core)
    to_root = dot("san,snp->sap", lower_to_root, lower_block).sum(axis=0)

    middle_solved = leaf_scatter(dot("smn,snp->smp", middle_inverse, middle_input)).astype(BF16)
    middle_block = leaf_gather(middle_solved).reshape(2, 1024, probes)
    to_root = to_root + dot("san,snp->sap", middle_to_root, middle_block).sum(axis=0)
    root_sum = row_half_sum(to_root.reshape(2, 256, probes), core)
    root_half = (lax.dynamic_index_in_dim(root_base, core, axis=0, keepdims=False) - root_sum).astype(BF16)
    root_input = both_halves(root_half, core).reshape(512, probes)

    root_solved = leaf_scatter(dot("mn,np->mp", root_inverse, root_input)).astype(BF16)
    root_rows = leaf_gather(root_solved)
    root_half = row_half_sum(dot("mn,mp->np", root_inverse, root_rows).reshape(2, 256, probes), core).astype(BF16)
    root_columns = both_halves(root_half, core).reshape(512, probes)

    middle_drop = leaf_scatter(dot("san,ap->snp", middle_to_root, root_columns))
    middle_reduced = (middle_solved.astype(F32) - middle_drop).astype(BF16)
    middle_rows = leaf_gather(middle_reduced).reshape(2, 1024, probes)
    middle_half = row_half_sum(dot("smn,smp->snp", middle_inverse, middle_rows), core).astype(BF16)
    middle_columns = both_halves(middle_half, core)

    lower_drop = dot("san,ap->snp", lower_to_root, root_columns)
    lower_drop = lower_drop + dot(
        "qsan,qap->qsnp", lower_to_middle.reshape(2, 2, 256, 512), middle_columns
    ).reshape(4, 512, probes)
    lower_reduced = (lower_solved.astype(F32) - leaf_scatter(lower_drop)).astype(BF16)
    lower_rows = z_gather(lower_reduced)
    lower_half = row_half_sum(dot("mn,mp->np", lower_square, lower_rows).reshape(2, 256, probes), core)
    lower_columns = both_halves(lower_half.astype(BF16), core).reshape(4, 128, probes)

    stacked = jnp.where(
        y < 2,
        lower_columns.reshape(4, 2, HALF, probes),
        jnp.where(
            y == 2,
            middle_columns.reshape(4, 2, HALF, probes),
            root_columns.reshape(4, 2, HALF, probes),
        ),
    )
    table = lax.dynamic_index_in_dim(stacked, core, axis=1, keepdims=False)
    sent = jnp.sum(chosen[:, :, None, None] * table[:, None].astype(F32), axis=0).astype(BF16)
    ancestor = jnp.sum(swap(sent, LEAF).astype(F32), axis=0).astype(BF16)
    leaf_back = row_scatter(dot("kb,kp->bp", panel, ancestor), core)
    leaf_reduced = (leaf_solved.astype(F32) - leaf_back).astype(BF16)
    leaf_solution = row_scatter(dot("ab,ap->bp", inverse, leaf_reduced), core).astype(BF16)

    own_rows = lax.dynamic_slice_in_dim(lower_columns, row * 16, 16, axis=1)
    by_separator = [own_rows[0]] + [shift(own_rows[step], "x", -step) for step in (1, 2, 3)]
    lower_solution = lax.dynamic_slice_in_dim(jnp.stack(by_separator + by_separator), (4 - x) % 4, 4, axis=0)
    middle_solution = lax.dynamic_slice_in_dim(middle_columns, row * 32, 32, axis=1)
    root_solution = lax.dynamic_slice_in_dim(root_columns, row * 64, 64, axis=0)
    return (leaf_solution[None], lower_solution, middle_solution, root_solution)


def solution(mesh):
    fine = Mesh(mesh.devices.reshape(4, 8, 4, 2), ("x", "z", "y", "core"))
    every = LEAF + ROW
    return jax.shard_map(
        body,
        mesh=fine,
        in_specs=(
            P(LEAF, ROW, None),
            P(None, every, None),
            P(None, every, None),
            P(every, None),
            P(LEAF, ROW, None),
            P(None, ROW, LEAF),
            P(None, ROW, LEAF),
            P(ROW, LEAF),
            P(LEAF, ROW, None),
            P(None, LEAF, ROW),
            P(None, LEAF, ROW),
            P(None, LEAF, ROW),
            P(),
            P(),
        ),
        out_specs=(
            P(LEAF, ROW, None),
            P(None, every, None),
            P(None, every, None),
            P(every, None),
        ),
        check_vma=False,
    )
```

```python
import jax
import jax.numpy as jnp
from jax import lax
from jax.experimental import pallas as pl
from jax.experimental.pallas import tpu as pltpu
from jax.sharding import Mesh, PartitionSpec as P

LEAF = ("x", "z")
ROW = ("y", "core")
LEAVES = 32
ROWS = 8
HALF = 64
F32 = jnp.float32
BF16 = jnp.bfloat16


def swap(pieces, axes):
    return lax.all_to_all(pieces, axes, split_axis=0, concat_axis=0, tiled=True)


def total(pieces):
    return jnp.sum(pieces.astype(F32), axis=0)


def copies(piece, count):
    return jnp.broadcast_to(piece[None], (count,) + piece.shape)


def leaf_terms(partial):
    return swap(partial.reshape(LEAVES, HALF, -1), LEAF)


def leaf_gather(piece):
    return swap(copies(piece.astype(BF16), LEAVES), LEAF)


def z_terms(partial):
    return swap(partial.reshape(8, HALF, -1), "z")


def z_gather(piece):
    return swap(copies(piece, 8), "z").reshape((-1,) + piece.shape[1:])


def shift(piece, axis, step):
    return lax.ppermute(piece, axis, [(i, (i + step) % 4) for i in range(4)])


def both_cores(piece):
    return lax.all_gather(piece, "core", axis=0, tiled=False)


def row_gather(piece):
    return both_cores(swap(copies(piece, 4), "y"))


def row_half_sum(partial, core):
    halves = lax.dynamic_slice_in_dim(both_cores(partial), core * 256, 256, axis=1)
    pair = total(halves).astype(BF16)
    others = [shift(pair, "y", step) for step in (1, 2, 3)]
    return sum([piece.astype(F32) for piece in others], pair.astype(F32))


def row_scatter(partial, core):
    halves = partial.reshape(4, 2, 256, -1)
    mine = jnp.where(core == 0, halves[:, 0], halves[:, 1])
    theirs = jnp.where(core == 0, halves[:, 1], halves[:, 0])
    pair = mine.astype(F32) + lax.ppermute(theirs, "core", [(0, 1), (1, 0)]).astype(F32)
    return total(swap(pair.astype(BF16), "y"))


def product(left, right):
    return jnp.dot(left, right, preferred_element_type=F32)


LIMITS = pltpu.CompilerParams(vmem_limit_bytes=12 * 1024 * 1024)


def forward(matrix, columns, rows_at_once=512):
    count, rows, depth = matrix.shape
    probes = columns.shape[-1]
    step = min(rows, rows_at_once)

    def kernel(matrix_ref, columns_ref, out_ref):
        out_ref[0] = product(matrix_ref[0], columns_ref[0]).astype(BF16)

    return pl.pallas_call(
        kernel,
        out_shape=jax.ShapeDtypeStruct((count, rows, probes), BF16),
        grid=(count, rows // step),
        in_specs=[
            pl.BlockSpec((1, step, depth), lambda s, m: (s, m, 0)),
            pl.BlockSpec((1, depth, probes), lambda s, m: (s, 0, 0)),
        ],
        out_specs=pl.BlockSpec((1, step, probes), lambda s, m: (s, m, 0)),
        compiler_params=LIMITS,
        name="forward",
    )(matrix, columns)


def forward_total(matrix, columns, start, group, dtype):
    count, rows, depth = matrix.shape
    probes = columns.shape[-1]

    def kernel(matrix_ref, columns_ref, start_ref, out_ref, sum_ref):
        member = pl.program_id(0) % group

        @pl.when(member == 0)
        def _():
            sum_ref[...] = start_ref[0]

        sum_ref[...] += product(matrix_ref[0], columns_ref[0])

        @pl.when(member == group - 1)
        def _():
            out_ref[0] = sum_ref[...].astype(dtype)

    in_specs = [
        pl.BlockSpec((1, rows, depth), lambda s: (s, 0, 0)),
        pl.BlockSpec((1, depth, probes), lambda s: (s, 0, 0)),
        pl.BlockSpec((1, rows, probes), lambda s: (s // group, 0, 0)),
    ]
    return pl.pallas_call(
        kernel,
        out_shape=jax.ShapeDtypeStruct((count // group, rows, probes), dtype),
        grid=(count,),
        in_specs=in_specs,
        out_specs=pl.BlockSpec((1, rows, probes), lambda s: (s // group, 0, 0)),
        scratch_shapes=[pltpu.VMEM((rows, probes), F32)],
        compiler_params=LIMITS,
        name="forward_total",
    )(matrix, columns, start)


def backward(matrix, rows_in, depth_at_once=512):
    count, depth, width = matrix.shape
    probes = rows_in.shape[-1]
    step = min(depth, depth_at_once)
    steps = depth // step

    def kernel(matrix_ref, rows_ref, out_ref, sum_ref):
        at = pl.program_id(1)

        @pl.when(at == 0)
        def _():
            sum_ref[...] = jnp.zeros_like(sum_ref)

        sum_ref[...] += product(rows_ref[0].T, matrix_ref[0])

        @pl.when(at == steps - 1)
        def _():
            out_ref[0] = sum_ref[...].T.astype(BF16)

    return pl.pallas_call(
        kernel,
        out_shape=jax.ShapeDtypeStruct((count, width, probes), BF16),
        grid=(count, steps),
        in_specs=[
            pl.BlockSpec((1, step, width), lambda s, m: (s, m, 0)),
            pl.BlockSpec((1, step, probes), lambda s, m: (s, m, 0)),
        ],
        out_specs=pl.BlockSpec((1, width, probes), lambda s, m: (s, 0, 0)),
        scratch_shapes=[pltpu.VMEM((probes, width), F32)],
        compiler_params=LIMITS,
        name="backward",
    )(matrix, rows_in)


def backward_lower(to_middle, middle_rows, to_root, root_rows):
    count, middle_depth, width = to_middle.shape
    root_depth = to_root.shape[1]
    probes = root_rows.shape[-1]

    def kernel(middle_ref, middle_rows_ref, root_ref, root_rows_ref, out_ref):
        both = product(root_rows_ref[...].T, root_ref[0]) + product(middle_rows_ref[0].T, middle_ref[0])
        out_ref[0] = both.T.astype(BF16)

    return pl.pallas_call(
        kernel,
        out_shape=jax.ShapeDtypeStruct((count, width, probes), BF16),
        grid=(count,),
        in_specs=[
            pl.BlockSpec((1, middle_depth, width), lambda s: (s, 0, 0)),
            pl.BlockSpec((1, middle_depth, probes), lambda s: (s // 2, 0, 0)),
            pl.BlockSpec((1, root_depth, width), lambda s: (s, 0, 0)),
            pl.BlockSpec((root_depth, probes), lambda s: (0, 0)),
        ],
        out_specs=pl.BlockSpec((1, width, probes), lambda s: (s, 0, 0)),
        compiler_params=LIMITS,
        name="backward_lower",
    )(to_middle, middle_rows, to_root, root_rows)


def pieces_product(matrix, held, times):
    rows, probes = matrix.shape[0], held.shape[-1]

    def kernel(matrix_ref, held_ref, out_ref):
        result = jnp.zeros((rows, probes), F32)
        for y in range(4):
            for core in range(2):
                at = (2 * y + core) * 256
                result += product(matrix_ref[:, at : at + 256], held_ref[core, y])
        rounded = result.astype(BF16)
        for copy in range(times):
            out_ref[copy] = rounded

    return pl.pallas_call(
        kernel,
        out_shape=jax.ShapeDtypeStruct((times, rows, probes), BF16),
        grid=(1,),
        in_specs=[
            pl.BlockSpec((rows, matrix.shape[1]), lambda i: (0, 0)),
            pl.BlockSpec((2, 4, 256, probes), lambda i: (0, 0, 0, 0)),
        ],
        out_specs=pl.BlockSpec((times, rows, probes), lambda i: (0, 0, 0)),
        compiler_params=LIMITS,
        name="pieces_product",
    )(matrix, held)


def body(
    leaf_probes,
    lower_probes,
    middle_probes,
    root_probes,
    leaf_inverse,
    lower_inverse,
    middle_inverse,
    root_inverse,
    leaf_panel,
    lower_to_middle,
    lower_to_root,
    middle_to_root,
    leaf_parent,
    leaf_blocks,
):
    x = lax.axis_index("x")
    z = lax.axis_index("z")
    leaf = x * 8 + z
    y = lax.axis_index("y")
    core = lax.axis_index("core")
    row = y * 2 + core
    probes = leaf_probes.shape[-1]
    inverse = leaf_inverse[0]
    panel = leaf_panel[0]

    lower_held = jnp.concatenate([lower_inverse, lower_probes], axis=1)
    leaving = [lax.dynamic_index_in_dim(lower_held, (x + step) % 4, axis=0, keepdims=False) for step in range(4)]
    leaf_probes, leaving = lax.optimization_barrier((leaf_probes, leaving))
    lower_tiles = [leaving[0]] + [shift(leaving[step], "x", step) for step in (1, 2, 3)]

    block = lax.dynamic_index_in_dim(leaf_blocks, y, axis=1, keepdims=False)
    parent = leaf_parent
    slot = jnp.where(
        y < 2,
        jnp.where((parent == x) & (block % 8 == z), (x + 4 - block // 8) % 4, -1),
        jnp.where(
            y == 2,
            jnp.where(block // 2 == leaf, (parent // 2) * 2 + block % 2, -1),
            jnp.where(block // 4 == leaf, block % 4, -1),
        ),
    )
    chosen = (slot[None, :] == jnp.arange(4, dtype=jnp.int32)[:, None]).astype(F32)

    held = row_gather(leaf_probes[0])
    leaf_solved = pieces_product(inverse, held, 1)[0]
    updates = pieces_product(panel, row_gather(leaf_solved), LEAVES)
    received, lower_tiles = lax.optimization_barrier((swap(updates, LEAF), lower_tiles))
    lower_square = jnp.concatenate([tile[:512] for tile in lower_tiles], axis=1)[None]
    lower_pieces = jnp.concatenate([tile[512:] for tile in lower_tiles])
    received = received.astype(F32)
    landed = jnp.sum(chosen[:, :, None, None] * received[None], axis=1).astype(BF16)
    by_level = swap(copies(jnp.concatenate([landed.reshape(-1, probes), lower_pieces]), 4), "y")
    added = by_level[:, :256].reshape(4, 4, HALF, probes)
    lower_added = (added[0].astype(F32) + added[1].astype(F32)).astype(BF16)
    by_half = both_cores(jnp.concatenate([lower_added, by_level[:, 256:]]))
    lower_added = by_half[:, :4].transpose(1, 0, 2, 3).reshape(4, 128, probes)
    lower_own = by_half[:, 4:].reshape(2, 4, 4, 16, probes).transpose(2, 1, 0, 3, 4).reshape(4, 128, probes)
    lower_input = (lower_own.astype(F32) - lower_added.astype(F32)).astype(BF16).reshape(1, 512, probes)

    half_ids = lax.broadcasted_iota(jnp.int32, (1, 2, 1, 1), 1)
    row_ids = lax.broadcasted_iota(jnp.int32, (1, ROWS, 1, 1), 1)

    def contribution(level, own_probes):
        placed = jnp.where((half_ids == core) & (y == level), landed[:, None].astype(F32), 0.0)
        own = jnp.where(row_ids == row, own_probes[:, None].astype(F32), 0.0)
        return placed.reshape(own_probes.shape[0], -1, probes) - own.reshape(own_probes.shape[0], -1, probes)

    middle_start = contribution(2, middle_probes)
    root_start = contribution(3, root_probes[None])

    lower_terms = z_terms(forward(lower_square, lower_input))
    lower_gathered = leaf_gather(total(lower_terms))
    lower_solved = lax.dynamic_index_in_dim(lower_gathered, leaf, axis=0, keepdims=False)
    lower_block = lower_gathered.reshape(4, 512, probes)
    to_middle = forward_total(lower_to_middle, lower_block, middle_start, 2, BF16).reshape(512, probes)
    middle_input = both_cores((-row_half_sum(to_middle, core)).astype(BF16))
    to_root = forward_total(lower_to_root, lower_block, root_start, 4, F32)

    middle_terms = leaf_terms(forward(middle_inverse, middle_input))
    middle_gathered = leaf_gather(total(middle_terms))
    middle_solved = lax.dynamic_index_in_dim(middle_gathered, leaf, axis=0, keepdims=False)
    middle_block = middle_gathered.reshape(2, 1024, probes)
    to_root = forward_total(middle_to_root, middle_block, to_root, 2, BF16).reshape(512, probes)
    root_input = both_cores((-row_half_sum(to_root, core)).astype(BF16)).reshape(1, 512, probes)

    root_terms = leaf_terms(forward(root_inverse[None], root_input))
    root_rows = leaf_gather(total(root_terms)).reshape(1, 2048, probes)
    root_half = row_half_sum(backward(root_inverse[None], root_rows)[0], core).astype(BF16)
    root_columns = both_cores(root_half).reshape(512, probes)

    middle_drop = leaf_terms(backward(middle_to_root, jnp.broadcast_to(root_columns[None], (2, 512, probes))))
    middle_rows = leaf_gather(middle_solved.astype(F32) - total(middle_drop)).reshape(2, 1024, probes)
    middle_half = row_half_sum(backward(middle_inverse, middle_rows).reshape(512, probes), core).astype(BF16)
    middle_columns = both_cores(middle_half)

    lower_drop = backward_lower(lower_to_middle, middle_columns, lower_to_root, root_columns)
    lower_rows = z_gather((lower_solved.astype(F32) - total(leaf_terms(lower_drop))).astype(BF16))
    lower_half = row_half_sum(backward(lower_square, lower_rows[None])[0], core)
    lower_columns = both_cores(lower_half.astype(BF16)).reshape(4, 128, probes)

    stacked = jnp.where(
        y < 2,
        lower_columns.reshape(4, 2, HALF, probes),
        jnp.where(
            y == 2,
            middle_columns.reshape(4, 2, HALF, probes),
            root_columns.reshape(4, 2, HALF, probes),
        ),
    )
    table = lax.dynamic_index_in_dim(stacked, core, axis=1, keepdims=False)
    sent = jnp.sum(chosen[:, :, None, None] * table[:, None].astype(F32), axis=0).astype(BF16)
    ancestor = total(swap(sent, LEAF)).astype(BF16)
    leaf_back = row_scatter(backward(panel[None], ancestor[None])[0], core)
    leaf_reduced = (leaf_solved.astype(F32) - leaf_back).astype(BF16)
    leaf_solution = row_scatter(backward(inverse[None], leaf_reduced[None])[0], core).astype(BF16)

    own_rows = lax.dynamic_slice_in_dim(lower_columns, row * 16, 16, axis=1)
    by_separator = [own_rows[0]] + [shift(own_rows[step], "x", -step) for step in (1, 2, 3)]
    lower_solution = lax.dynamic_slice_in_dim(jnp.stack(by_separator + by_separator), (4 - x) % 4, 4, axis=0)
    middle_solution = lax.dynamic_slice_in_dim(middle_columns, row * 32, 32, axis=1)
    root_solution = lax.dynamic_slice_in_dim(root_columns, row * 64, 64, axis=0)
    return (leaf_solution[None], lower_solution, middle_solution, root_solution)


def solution(mesh):
    fine = Mesh(mesh.devices.reshape(4, 8, 4, 2), ("x", "z", "y", "core"))
    every = LEAF + ROW
    return jax.shard_map(
        body,
        mesh=fine,
        in_specs=(
            P(LEAF, ROW, None),
            P(None, every, None),
            P(None, every, None),
            P(every, None),
            P(LEAF, ROW, None),
            P(None, ROW, LEAF),
            P(None, ROW, LEAF),
            P(ROW, LEAF),
            P(LEAF, ROW, None),
            P(None, LEAF, ROW),
            P(None, LEAF, ROW),
            P(None, LEAF, ROW),
            P(),
            P(),
        ),
        out_specs=(
            P(LEAF, ROW, None),
            P(None, every, None),
            P(None, every, None),
            P(every, None),
        ),
        check_vma=False,
    )
```

```python
import jax
import jax.numpy as jnp
from jax import lax
from jax.experimental import pallas as pl
from jax.experimental.pallas import tpu as pltpu
from jax.sharding import Mesh, PartitionSpec as P

LEAF = ("x", "z")
ROW = ("y", "core")
LEAVES = 32
ROWS = 8
HALF = 64
BLOCK = 128
F32 = jnp.float32
BF16 = jnp.bfloat16


def swap(pieces, axes):
    return lax.all_to_all(pieces, axes, split_axis=0, concat_axis=0, tiled=True)


def total(pieces):
    return jnp.sum(pieces.astype(F32), axis=0)


def copies(piece, count):
    return jnp.broadcast_to(piece[None], (count,) + piece.shape)


def leaf_terms(partial):
    return swap(partial.reshape(LEAVES, HALF, -1), LEAF)


def leaf_gather(piece):
    return swap(copies(piece.astype(BF16), LEAVES), LEAF)


def cut(array, start, size, axis):
    return lax.dynamic_slice_in_dim(array, start.astype(jnp.uint32), size, axis=axis)


def z_terms(partial):
    return swap(partial.reshape(8, HALF, -1), "z")


def z_gather(piece):
    return swap(copies(piece, 8), "z").reshape((-1,) + piece.shape[1:])


def shift(piece, axis, step):
    return lax.ppermute(piece, axis, [(i, (i + step) % 4) for i in range(4)])


def take(array, index, axis):
    return lax.dynamic_index_in_dim(array, index.astype(jnp.uint32), axis=axis, keepdims=False)


def both_cores(piece):
    return lax.all_gather(piece, "core", axis=0, tiled=False)


def row_gather(piece):
    return both_cores(swap(copies(piece, 4), "y"))


def row_half_sum(partial, core, beside=None):
    pair = total(take(both_cores(partial.reshape(2, 256, -1)), core, 1)).astype(BF16)
    others = [shift(pair, "y", step) for step in (1, 2, 3)]
    result = sum([piece.astype(F32) for piece in others], pair.astype(F32))
    return result if beside is None else (result, beside(pair))


def row_scatter(partial, core):
    halves = partial.reshape(4, 2, 256, -1)
    mine = jnp.where(core == 0, halves[:, 0], halves[:, 1])
    theirs = jnp.where(core == 0, halves[:, 1], halves[:, 0])
    pair = mine.astype(F32) + lax.ppermute(theirs, "core", [(0, 1), (1, 0)]).astype(F32)
    return total(swap(pair.astype(BF16), "y"))


def product(left, right):
    return jnp.dot(left, right, preferred_element_type=F32)


LIMITS = pltpu.CompilerParams(vmem_limit_bytes=12 * 1024 * 1024)


def forward(matrix, columns, rows_at_once=512):
    count, rows, depth = matrix.shape
    probes = columns.shape[-1]
    step = min(rows, rows_at_once)

    def kernel(matrix_ref, columns_ref, out_ref):
        out_ref[0] = product(matrix_ref[0], columns_ref[0]).astype(BF16)

    return pl.pallas_call(
        kernel,
        out_shape=jax.ShapeDtypeStruct((count, rows, probes), BF16),
        grid=(count, rows // step),
        in_specs=[
            pl.BlockSpec((1, step, depth), lambda s, m: (s, m, 0)),
            pl.BlockSpec((1, depth, probes), lambda s, m: (s, 0, 0)),
        ],
        out_specs=pl.BlockSpec((1, step, probes), lambda s, m: (s, m, 0)),
        compiler_params=LIMITS,
        name="forward",
    )(matrix, columns)


def forward_total(matrix, columns, position, landed, own_probes, carried, dtype):
    count, rows, depth = matrix.shape
    probes = columns.shape[-1]
    groups = (own_probes if carried is None else carried).shape[0]
    group = count // groups
    slots = rows // BLOCK

    parts = 2
    part = rows // parts

    def kernel(position_ref, matrix_ref, columns_ref, *refs):
        out_ref, held_ref, sems, sum_ref = refs[-4:]
        moves = {}
        for member in range(count):
            for piece in range(parts):
                at = pl.ds(piece * part, part)
                moves[member, piece] = pltpu.make_async_copy(
                    matrix_ref.at[member, at], held_ref.at[member, at], sems.at[member * parts + piece]
                )
                moves[member, piece].start()
        for unit in range(groups):
            for piece in range(parts):
                at = slice(piece * part, piece * part + part)
                result = refs[0][unit, at].astype(F32) if carried is not None else jnp.zeros((part, probes), F32)
                for member in range(unit * group, unit * group + group):
                    moves[member, piece].wait()
                    result += product(held_ref[member, at], columns_ref[member])
                if carried is not None:
                    out_ref[unit, at] = result.astype(dtype)
                else:
                    sum_ref[unit, at] = result
            if carried is None:
                landed_ref, own_ref = refs[:2]
                here, core, row = position_ref[0], position_ref[1], position_ref[2]
                for slot in range(slots):
                    at = pl.ds(pl.multiple_of(slot * BLOCK + core * HALF, HALF), HALF)
                    sum_ref[unit, at, :] += jnp.where(here > 0, landed_ref[unit * slots + slot].astype(F32), 0.0)
                own = rows // ROWS
                at = pl.ds(pl.multiple_of(row * own, own), own)
                sum_ref[unit, at, :] -= own_ref[unit].astype(F32)
                out_ref[unit] = sum_ref[unit].astype(dtype)

    vmem = pl.BlockSpec(memory_space=pltpu.VMEM)
    operands = (landed, own_probes) if carried is None else (carried,)
    scratch = [
        pltpu.VMEM((count, rows, depth), BF16),
        pltpu.SemaphoreType.DMA((count * parts,)),
        pltpu.VMEM((groups, rows, probes), F32),
    ]
    return pl.pallas_call(
        kernel,
        out_shape=jax.ShapeDtypeStruct((groups, rows, probes), dtype),
        in_specs=[pl.BlockSpec(memory_space=pltpu.SMEM), pl.BlockSpec(memory_space=pltpu.HBM), vmem]
        + [vmem] * len(operands),
        out_specs=vmem,
        scratch_shapes=scratch,
        compiler_params=LIMITS,
        name="forward_total",
    )(position, pltpu.with_memory_space_constraint(matrix, pltpu.HBM), columns, *operands)


def backward(matrix, rows_in, depth_at_once=512):
    count, depth, width = matrix.shape
    probes = rows_in.shape[-1]
    step = min(depth, depth_at_once)
    steps = depth // step

    def kernel(matrix_ref, rows_ref, out_ref, sum_ref):
        at = pl.program_id(1)

        @pl.when(at == 0)
        def _():
            sum_ref[...] = jnp.zeros_like(sum_ref)

        sum_ref[...] += product(rows_ref[0].T, matrix_ref[0])

        @pl.when(at == steps - 1)
        def _():
            out_ref[0] = sum_ref[...].T.astype(BF16)

    return pl.pallas_call(
        kernel,
        out_shape=jax.ShapeDtypeStruct((count, width, probes), BF16),
        grid=(count, steps),
        in_specs=[
            pl.BlockSpec((1, step, width), lambda s, m: (s, m, 0)),
            pl.BlockSpec((1, step, probes), lambda s, m: (s, m, 0)),
        ],
        out_specs=pl.BlockSpec((1, width, probes), lambda s, m: (s, 0, 0)),
        scratch_shapes=[pltpu.VMEM((probes, width), F32)],
        compiler_params=LIMITS,
        name="backward",
    )(matrix, rows_in)


def backward_lower(to_middle, middle_rows, to_root, root_rows):
    count, middle_depth, width = to_middle.shape
    root_depth = to_root.shape[1]
    probes = root_rows.shape[-1]

    def kernel(middle_ref, middle_rows_ref, root_ref, root_rows_ref, out_ref):
        both = product(root_rows_ref[...].T, root_ref[0]) + product(middle_rows_ref[0].T, middle_ref[0])
        out_ref[0] = both.T.astype(BF16)

    return pl.pallas_call(
        kernel,
        out_shape=jax.ShapeDtypeStruct((count, width, probes), BF16),
        grid=(count,),
        in_specs=[
            pl.BlockSpec((1, middle_depth, width), lambda s: (s, 0, 0)),
            pl.BlockSpec((1, middle_depth, probes), lambda s: (s // 2, 0, 0)),
            pl.BlockSpec((1, root_depth, width), lambda s: (s, 0, 0)),
            pl.BlockSpec((root_depth, probes), lambda s: (0, 0)),
        ],
        out_specs=pl.BlockSpec((1, width, probes), lambda s: (s, 0, 0)),
        compiler_params=LIMITS,
        name="backward_lower",
    )(to_middle, middle_rows, to_root, root_rows)


def pieces_product(matrix, held, times):
    rows, probes = matrix.shape[0], held.shape[-1]

    def kernel(matrix_ref, held_ref, out_ref):
        result = jnp.zeros((rows, probes), F32)
        for y in range(4):
            for core in range(2):
                at = (2 * y + core) * 256
                result += product(matrix_ref[:, at : at + 256], held_ref[core, y])
        rounded = result.astype(BF16)
        for copy in range(times):
            out_ref[copy] = rounded

    return pl.pallas_call(
        kernel,
        out_shape=jax.ShapeDtypeStruct((times, rows, probes), BF16),
        grid=(1,),
        in_specs=[
            pl.BlockSpec((rows, matrix.shape[1]), lambda i: (0, 0)),
            pl.BlockSpec((2, 4, 256, probes), lambda i: (0, 0, 0, 0)),
        ],
        out_specs=pl.BlockSpec((times, rows, probes), lambda i: (0, 0, 0)),
        compiler_params=LIMITS,
        name="pieces_product",
    )(matrix, held)


def body(
    leaf_probes,
    lower_probes,
    middle_probes,
    root_probes,
    leaf_inverse,
    lower_inverse,
    middle_inverse,
    root_inverse,
    leaf_panel,
    lower_to_middle,
    lower_to_root,
    middle_to_root,
    leaf_parent,
    leaf_blocks,
):
    x = lax.axis_index("x")
    z = lax.axis_index("z")
    leaf = x * 8 + z
    y = lax.axis_index("y")
    core = lax.axis_index("core")
    row = y * 2 + core
    probes = leaf_probes.shape[-1]
    inverse = leaf_inverse[0]
    panel = leaf_panel[0]

    block = take(leaf_blocks, y, 1)
    parent = leaf_parent
    slot = jnp.where(
        y < 2,
        jnp.where((parent == x) & (block % 8 == z), (x + 4 - block // 8) % 4, -1),
        jnp.where(
            y == 2,
            jnp.where(block // 2 == leaf, (parent // 2) * 2 + block % 2, -1),
            jnp.where(block // 4 == leaf, block % 4, -1),
        ),
    )
    chosen = (slot[None, :] == jnp.arange(4, dtype=jnp.int32)[:, None]).astype(F32)

    held = row_gather(leaf_probes[0])
    leaf_solved = pieces_product(inverse, held, 1)[0]
    updates = pieces_product(panel, row_gather(leaf_solved), LEAVES)
    updates, tiles, pieces = lax.optimization_barrier((updates, lower_inverse, lower_probes))
    lower_held = jnp.concatenate([tiles, pieces], axis=1)
    leaving = [take(lower_held, (x + step) % 4, 0) for step in range(4)]
    lower_tiles = [leaving[0]] + [shift(leaving[step], "x", step) for step in (1, 2, 3)]
    received, lower_tiles = lax.optimization_barrier((swap(updates, LEAF), lower_tiles))
    lower_square = jnp.concatenate([tile[:512] for tile in lower_tiles], axis=1)[None]
    lower_pieces = jnp.concatenate([tile[512:] for tile in lower_tiles])
    received = received.astype(F32)
    landed = jnp.sum(chosen[:, :, None, None] * received[None], axis=1).astype(BF16)
    by_level = swap(copies(jnp.concatenate([landed.reshape(-1, probes), lower_pieces]), 4), "y")
    added = by_level[:, :256].reshape(4, 4, HALF, probes)
    lower_added = (added[0].astype(F32) + added[1].astype(F32)).astype(BF16)
    by_half = both_cores(jnp.concatenate([lower_added, by_level[:, 256:]]))
    lower_added = by_half[:, :4].transpose(1, 0, 2, 3).reshape(4, 128, probes)
    lower_own = by_half[:, 4:].reshape(2, 4, 4, 16, probes).transpose(2, 1, 0, 3, 4).reshape(4, 128, probes)
    lower_input = (lower_own.astype(F32) - lower_added.astype(F32)).astype(BF16).reshape(1, 512, probes)

    lower_terms = z_terms(forward(lower_square, lower_input))
    lower_gathered = leaf_gather(total(lower_terms))
    lower_solved = take(lower_gathered, leaf, 0)
    lower_block = lower_gathered.reshape(4, 512, probes)

    def at_level(level):
        return jnp.stack([(y == level).astype(jnp.int32), core, row])

    def early_root(pair):
        block, _ = lax.optimization_barrier((lower_block, pair))
        return forward_total(lower_to_root, block, at_level(3), landed, root_probes[None], None, F32)

    to_middle = forward_total(lower_to_middle, lower_block, at_level(2), landed, middle_probes, None, BF16).reshape(512, probes)
    middle_half, to_root = row_half_sum(to_middle, core, early_root)
    middle_half, to_root = lax.optimization_barrier((middle_half, to_root))
    middle_input = both_cores((-middle_half).astype(BF16))

    middle_terms = leaf_terms(forward(middle_inverse, middle_input))
    middle_gathered = leaf_gather(total(middle_terms))
    middle_solved = take(middle_gathered, leaf, 0)
    middle_block = middle_gathered.reshape(2, 1024, probes)
    to_root = forward_total(middle_to_root, middle_block, at_level(3), None, None, to_root, BF16).reshape(512, probes)
    root_input = both_cores((-row_half_sum(to_root, core)).astype(BF16)).reshape(1, 512, probes)

    root_terms = leaf_terms(forward(root_inverse[None], root_input))
    root_rows = leaf_gather(total(root_terms)).reshape(1, 2048, probes)
    root_half = row_half_sum(backward(root_inverse[None], root_rows)[0], core).astype(BF16)
    root_columns = both_cores(root_half).reshape(512, probes)

    middle_drop = leaf_terms(backward(middle_to_root, jnp.broadcast_to(root_columns[None], (2, 512, probes))))
    middle_rows = leaf_gather(middle_solved.astype(F32) - total(middle_drop)).reshape(2, 1024, probes)
    middle_half = row_half_sum(backward(middle_inverse, middle_rows).reshape(512, probes), core).astype(BF16)
    middle_columns = both_cores(middle_half)

    lower_drop = backward_lower(lower_to_middle, middle_columns, lower_to_root, root_columns)
    lower_rows = z_gather((lower_solved.astype(F32) - total(leaf_terms(lower_drop))).astype(BF16))
    lower_half = row_half_sum(backward(lower_square, lower_rows[None])[0], core)
    lower_columns = both_cores(lower_half.astype(BF16)).reshape(4, 128, probes)

    stacked = jnp.where(
        y < 2,
        lower_columns.reshape(4, 2, HALF, probes),
        jnp.where(
            y == 2,
            middle_columns.reshape(4, 2, HALF, probes),
            root_columns.reshape(4, 2, HALF, probes),
        ),
    )
    table = take(stacked, core, 1)
    sent = jnp.sum(chosen[:, :, None, None] * table[:, None].astype(F32), axis=0).astype(BF16)
    ancestor = total(swap(sent, LEAF)).astype(BF16)
    leaf_back = row_scatter(backward(panel[None], ancestor[None])[0], core)
    leaf_reduced = (leaf_solved.astype(F32) - leaf_back).astype(BF16)
    leaf_solution = row_scatter(backward(inverse[None], leaf_reduced[None])[0], core).astype(BF16)

    own_rows = cut(lower_columns, row * 16, 16, 1)
    by_separator = [own_rows[0]] + [shift(own_rows[step], "x", -step) for step in (1, 2, 3)]
    lower_solution = cut(jnp.stack(by_separator + by_separator), (4 - x) % 4, 4, 0)
    middle_solution = cut(middle_columns, row * 32, 32, 1)
    root_solution = cut(root_columns, row * 64, 64, 0)
    return (leaf_solution[None], lower_solution, middle_solution, root_solution)


def solution(mesh):
    fine = Mesh(mesh.devices.reshape(4, 8, 4, 2), ("x", "z", "y", "core"))
    every = LEAF + ROW
    return jax.shard_map(
        body,
        mesh=fine,
        in_specs=(
            P(LEAF, ROW, None),
            P(None, every, None),
            P(None, every, None),
            P(every, None),
            P(LEAF, ROW, None),
            P(None, ROW, LEAF),
            P(None, ROW, LEAF),
            P(ROW, LEAF),
            P(LEAF, ROW, None),
            P(None, LEAF, ROW),
            P(None, LEAF, ROW),
            P(None, LEAF, ROW),
            P(),
            P(),
        ),
        out_specs=(
            P(LEAF, ROW, None),
            P(None, every, None),
            P(None, every, None),
            P(every, None),
        ),
        check_vma=False,
    )
```

```python
import jax
import jax.numpy as jnp
from jax import lax
from jax.experimental import pallas as pl
from jax.experimental.pallas import tpu as pltpu
from jax.sharding import Mesh, PartitionSpec as P

LEAF = ("x", "z")
ROW = ("y", "core")
LEAVES = 32
ROWS = 8
HALF = 64
BLOCK = 128
F32 = jnp.float32
BF16 = jnp.bfloat16


def swap(pieces, axes):
    return lax.all_to_all(pieces, axes, split_axis=0, concat_axis=0, tiled=True)


def total(pieces):
    return jnp.sum(pieces.astype(F32), axis=0)


def copies(piece, count):
    return jnp.broadcast_to(piece[None], (count,) + piece.shape)


def leaf_terms(partial):
    return swap(partial.reshape(LEAVES, HALF, -1), LEAF)


def leaf_gather(piece):
    return swap(copies(piece.astype(BF16), LEAVES), LEAF)


def cut(array, start, size, axis):
    return lax.dynamic_slice_in_dim(array, start.astype(jnp.uint32), size, axis=axis)


def z_terms(partial):
    return swap(partial.reshape(8, HALF, -1), "z")


def z_gather(piece):
    return swap(copies(piece, 8), "z").reshape((-1,) + piece.shape[1:])


def shift(piece, axis, step):
    return lax.ppermute(piece, axis, [(i, (i + step) % 4) for i in range(4)])


def take(array, index, axis):
    return lax.dynamic_index_in_dim(array, index.astype(jnp.uint32), axis=axis, keepdims=False)


def both_cores(piece):
    return lax.all_gather(piece, "core", axis=0, tiled=False)


def row_gather(piece):
    return both_cores(swap(copies(piece, 4), "y"))


def row_half_sum(partial, core, beside=None):
    pair = total(take(both_cores(partial.reshape(2, 256, -1)), core, 1)).astype(BF16)
    others = [shift(pair, "y", step) for step in (1, 2, 3)]
    result = sum([piece.astype(F32) for piece in others], pair.astype(F32))
    return result if beside is None else (result, beside(pair))


def row_scatter(partial, core):
    halves = partial.reshape(4, 2, 256, -1)
    mine = jnp.where(core == 0, halves[:, 0], halves[:, 1])
    theirs = jnp.where(core == 0, halves[:, 1], halves[:, 0])
    pair = mine.astype(F32) + lax.ppermute(theirs, "core", [(0, 1), (1, 0)]).astype(F32)
    return total(swap(pair.astype(BF16), "y"))


def product(left, right):
    return jnp.dot(left, right, preferred_element_type=F32)


LIMITS = pltpu.CompilerParams(vmem_limit_bytes=12 * 1024 * 1024)


def forward(matrix, columns, rows_at_once=512):
    count, rows, depth = matrix.shape
    probes = columns.shape[-1]
    step = min(rows, rows_at_once)

    def kernel(matrix_ref, columns_ref, out_ref):
        out_ref[0] = product(matrix_ref[0], columns_ref[0]).astype(BF16)

    return pl.pallas_call(
        kernel,
        out_shape=jax.ShapeDtypeStruct((count, rows, probes), BF16),
        grid=(count, rows // step),
        in_specs=[
            pl.BlockSpec((1, step, depth), lambda s, m: (s, m, 0)),
            pl.BlockSpec((1, depth, probes), lambda s, m: (s, 0, 0)),
        ],
        out_specs=pl.BlockSpec((1, step, probes), lambda s, m: (s, m, 0)),
        compiler_params=LIMITS,
        name="forward",
    )(matrix, columns)


def forward_total(matrix, columns, position, landed, own_probes, carried, dtype):
    count, rows, depth = matrix.shape
    probes = columns.shape[-1]
    groups = (own_probes if carried is None else carried).shape[0]
    group = count // groups
    slots = rows // BLOCK

    def kernel(position_ref, matrix_ref, columns_ref, *refs):
        out_ref, sum_ref = refs[-2:]
        member = pl.program_id(0) % group

        @pl.when(member == 0)
        def _():
            if carried is not None:
                sum_ref[...] = refs[0][0].astype(F32)
            else:
                landed_ref, own_ref = refs[:2]
                here, core, row = position_ref[0], position_ref[1], position_ref[2]
                sum_ref[...] = jnp.zeros_like(sum_ref)
                for slot in range(slots):
                    at = pl.ds(pl.multiple_of(slot * BLOCK + core * HALF, HALF), HALF)
                    sum_ref[at, :] += jnp.where(here > 0, landed_ref[slot].astype(F32), 0.0)
                own = rows // ROWS
                at = pl.ds(pl.multiple_of(row * own, own), own)
                sum_ref[at, :] -= own_ref[0].astype(F32)

        sum_ref[...] += product(matrix_ref[0], columns_ref[0])

        @pl.when(member == group - 1)
        def _():
            out_ref[0] = sum_ref[...].astype(dtype)

    in_specs = [
        pl.BlockSpec(memory_space=pltpu.SMEM),
        pl.BlockSpec((1, rows, depth), lambda s: (s, 0, 0)),
        pl.BlockSpec((1, depth, probes), lambda s: (s, 0, 0)),
    ]
    if carried is None:
        in_specs += [
            pl.BlockSpec((slots, HALF, probes), lambda s: (s // group, 0, 0)),
            pl.BlockSpec((1, rows // ROWS, probes), lambda s: (s // group, 0, 0)),
        ]
        operands = (landed, own_probes)
    else:
        in_specs += [pl.BlockSpec((1, rows, probes), lambda s: (s // group, 0, 0))]
        operands = (carried,)
    return pl.pallas_call(
        kernel,
        out_shape=jax.ShapeDtypeStruct((groups, rows, probes), dtype),
        grid=(count,),
        in_specs=in_specs,
        out_specs=pl.BlockSpec((1, rows, probes), lambda s: (s // group, 0, 0)),
        scratch_shapes=[pltpu.VMEM((rows, probes), F32)],
        compiler_params=LIMITS,
        name="forward_total",
    )(position, matrix, columns, *operands)


def backward(matrix, rows_in, depth_at_once=512):
    count, depth, width = matrix.shape
    probes = rows_in.shape[-1]
    step = min(depth, depth_at_once)
    steps = depth // step

    def kernel(matrix_ref, rows_ref, out_ref, sum_ref):
        at = pl.program_id(1)

        @pl.when(at == 0)
        def _():
            sum_ref[...] = jnp.zeros_like(sum_ref)

        sum_ref[...] += product(rows_ref[0].T, matrix_ref[0])

        @pl.when(at == steps - 1)
        def _():
            out_ref[0] = sum_ref[...].T.astype(BF16)

    return pl.pallas_call(
        kernel,
        out_shape=jax.ShapeDtypeStruct((count, width, probes), BF16),
        grid=(count, steps),
        in_specs=[
            pl.BlockSpec((1, step, width), lambda s, m: (s, m, 0)),
            pl.BlockSpec((1, step, probes), lambda s, m: (s, m, 0)),
        ],
        out_specs=pl.BlockSpec((1, width, probes), lambda s, m: (s, 0, 0)),
        scratch_shapes=[pltpu.VMEM((probes, width), F32)],
        compiler_params=LIMITS,
        name="backward",
    )(matrix, rows_in)


def backward_lower(to_middle, middle_rows, to_root, root_rows):
    count, middle_depth, width = to_middle.shape
    root_depth = to_root.shape[1]
    probes = root_rows.shape[-1]

    def kernel(middle_ref, middle_rows_ref, root_ref, root_rows_ref, out_ref):
        both = product(root_rows_ref[...].T, root_ref[0]) + product(middle_rows_ref[0].T, middle_ref[0])
        out_ref[0] = both.T.astype(BF16)

    return pl.pallas_call(
        kernel,
        out_shape=jax.ShapeDtypeStruct((count, width, probes), BF16),
        grid=(count,),
        in_specs=[
            pl.BlockSpec((1, middle_depth, width), lambda s: (s, 0, 0)),
            pl.BlockSpec((1, middle_depth, probes), lambda s: (s // 2, 0, 0)),
            pl.BlockSpec((1, root_depth, width), lambda s: (s, 0, 0)),
            pl.BlockSpec((root_depth, probes), lambda s: (0, 0)),
        ],
        out_specs=pl.BlockSpec((1, width, probes), lambda s: (s, 0, 0)),
        compiler_params=LIMITS,
        name="backward_lower",
    )(to_middle, middle_rows, to_root, root_rows)


def pieces_product(matrix, held, times):
    rows, probes = matrix.shape[0], held.shape[-1]

    def kernel(matrix_ref, held_ref, out_ref):
        result = jnp.zeros((rows, probes), F32)
        for y in range(4):
            for core in range(2):
                at = (2 * y + core) * 256
                result += product(matrix_ref[:, at : at + 256], held_ref[core, y])
        rounded = result.astype(BF16)
        for copy in range(times):
            out_ref[copy] = rounded

    return pl.pallas_call(
        kernel,
        out_shape=jax.ShapeDtypeStruct((times, rows, probes), BF16),
        grid=(1,),
        in_specs=[
            pl.BlockSpec((rows, matrix.shape[1]), lambda i: (0, 0)),
            pl.BlockSpec((2, 4, 256, probes), lambda i: (0, 0, 0, 0)),
        ],
        out_specs=pl.BlockSpec((times, rows, probes), lambda i: (0, 0, 0)),
        compiler_params=LIMITS,
        name="pieces_product",
    )(matrix, held)


def body(
    leaf_probes,
    lower_probes,
    middle_probes,
    root_probes,
    leaf_inverse,
    lower_inverse,
    middle_inverse,
    root_inverse,
    leaf_panel,
    lower_to_middle,
    lower_to_root,
    middle_to_root,
    leaf_parent,
    leaf_blocks,
):
    x = lax.axis_index("x")
    z = lax.axis_index("z")
    leaf = x * 8 + z
    y = lax.axis_index("y")
    core = lax.axis_index("core")
    row = y * 2 + core
    probes = leaf_probes.shape[-1]
    inverse = leaf_inverse[0]
    panel = leaf_panel[0]

    block = take(leaf_blocks, y, 1)
    parent = leaf_parent
    slot = jnp.where(
        y < 2,
        jnp.where((parent == x) & (block % 8 == z), (x + 4 - block // 8) % 4, -1),
        jnp.where(
            y == 2,
            jnp.where(block // 2 == leaf, (parent // 2) * 2 + block % 2, -1),
            jnp.where(block // 4 == leaf, block % 4, -1),
        ),
    )
    chosen = (slot[None, :] == jnp.arange(4, dtype=jnp.int32)[:, None]).astype(F32)

    held = row_gather(leaf_probes[0])
    solved_copies = pieces_product(inverse, held, 4)
    leaf_solved = solved_copies[0]
    updates = pieces_product(panel, both_cores(swap(solved_copies, "y")), LEAVES)
    updates, tiles, pieces = lax.optimization_barrier((updates, lower_inverse, lower_probes))
    lower_held = jnp.concatenate([tiles, pieces], axis=1)
    leaving = [take(lower_held, (x + step) % 4, 0) for step in range(4)]
    lower_tiles = [leaving[0]] + [shift(leaving[step], "x", step) for step in (1, 2, 3)]
    received, lower_tiles = lax.optimization_barrier((swap(updates, LEAF), lower_tiles))
    lower_square = jnp.concatenate([tile[:512] for tile in lower_tiles], axis=1)[None]
    lower_pieces = jnp.concatenate([tile[512:] for tile in lower_tiles])
    received = received.astype(F32)
    landed = jnp.sum(chosen[:, :, None, None] * received[None], axis=1).astype(BF16)
    by_level = swap(copies(jnp.concatenate([landed.reshape(-1, probes), lower_pieces]), 4), "y")
    added = by_level[:, :256].reshape(4, 4, HALF, probes)
    lower_added = (added[0].astype(F32) + added[1].astype(F32)).astype(BF16)
    by_half = both_cores(jnp.concatenate([lower_added, by_level[:, 256:]]))
    lower_added = by_half[:, :4].transpose(1, 0, 2, 3).reshape(4, 128, probes)
    lower_own = by_half[:, 4:].reshape(2, 4, 4, 16, probes).transpose(2, 1, 0, 3, 4).reshape(4, 128, probes)
    lower_input = (lower_own.astype(F32) - lower_added.astype(F32)).astype(BF16).reshape(1, 512, probes)

    lower_terms = z_terms(forward(lower_square, lower_input))
    lower_gathered = leaf_gather(total(lower_terms))
    lower_solved = take(lower_gathered, leaf, 0)
    lower_block = lower_gathered.reshape(4, 512, probes)

    def at_level(level):
        return jnp.stack([(y == level).astype(jnp.int32), core, row])

    def early_root(pair):
        block, _ = lax.optimization_barrier((lower_block, pair))
        return forward_total(lower_to_root, block, at_level(3), landed, root_probes[None], None, BF16)

    to_middle = forward_total(lower_to_middle, lower_block, at_level(2), landed, middle_probes, None, BF16).reshape(512, probes)
    middle_half, to_root = row_half_sum(to_middle, core, early_root)
    middle_half, to_root = lax.optimization_barrier((middle_half, to_root))
    middle_input = both_cores((-middle_half).astype(BF16))

    middle_terms = leaf_terms(forward(middle_inverse, middle_input))
    middle_gathered = leaf_gather(total(middle_terms))
    middle_solved = take(middle_gathered, leaf, 0)
    middle_block = middle_gathered.reshape(2, 1024, probes)
    to_root = forward_total(middle_to_root, middle_block, at_level(3), None, None, to_root, BF16).reshape(512, probes)
    root_input = both_cores((-row_half_sum(to_root, core)).astype(BF16)).reshape(1, 512, probes)

    root_terms = leaf_terms(forward(root_inverse[None], root_input))
    root_rows = leaf_gather(total(root_terms)).reshape(1, 2048, probes)
    root_half = row_half_sum(backward(root_inverse[None], root_rows)[0], core).astype(BF16)
    root_columns = both_cores(root_half).reshape(512, probes)

    middle_drop = leaf_terms(backward(middle_to_root, jnp.broadcast_to(root_columns[None], (2, 512, probes))))
    middle_rows = leaf_gather(middle_solved.astype(F32) - total(middle_drop)).reshape(2, 1024, probes)
    middle_half = row_half_sum(backward(middle_inverse, middle_rows).reshape(512, probes), core).astype(BF16)
    middle_columns = both_cores(middle_half)

    lower_drop = backward_lower(lower_to_middle, middle_columns, lower_to_root, root_columns)
    lower_rows = z_gather((lower_solved.astype(F32) - total(leaf_terms(lower_drop))).astype(BF16))
    lower_half = row_half_sum(backward(lower_square, lower_rows[None])[0], core)
    lower_columns = both_cores(lower_half.astype(BF16)).reshape(4, 128, probes)

    stacked = jnp.where(
        y < 2,
        lower_columns.reshape(4, 2, HALF, probes),
        jnp.where(
            y == 2,
            middle_columns.reshape(4, 2, HALF, probes),
            root_columns.reshape(4, 2, HALF, probes),
        ),
    )
    table = take(stacked, core, 1)
    sent = jnp.sum(chosen[:, :, None, None] * table[:, None].astype(F32), axis=0).astype(BF16)
    ancestor = total(swap(sent, LEAF)).astype(BF16)
    leaf_back = row_scatter(backward(panel[None], ancestor[None])[0], core)
    leaf_reduced = (leaf_solved.astype(F32) - leaf_back).astype(BF16)
    leaf_solution = row_scatter(backward(inverse[None], leaf_reduced[None])[0], core).astype(BF16)

    own_rows = cut(lower_columns, row * 16, 16, 1)
    by_separator = [own_rows[0]] + [shift(own_rows[step], "x", -step) for step in (1, 2, 3)]
    lower_solution = cut(jnp.stack(by_separator + by_separator), (4 - x) % 4, 4, 0)
    middle_solution = cut(middle_columns, row * 32, 32, 1)
    root_solution = cut(root_columns, row * 64, 64, 0)
    return (leaf_solution[None], lower_solution, middle_solution, root_solution)


def solution(mesh):
    fine = Mesh(mesh.devices.reshape(4, 8, 4, 2), ("x", "z", "y", "core"))
    every = LEAF + ROW
    return jax.shard_map(
        body,
        mesh=fine,
        in_specs=(
            P(LEAF, ROW, None),
            P(None, every, None),
            P(None, every, None),
            P(every, None),
            P(LEAF, ROW, None),
            P(None, ROW, LEAF),
            P(None, ROW, LEAF),
            P(ROW, LEAF),
            P(LEAF, ROW, None),
            P(None, LEAF, ROW),
            P(None, LEAF, ROW),
            P(None, LEAF, ROW),
            P(),
            P(),
        ),
        out_specs=(
            P(LEAF, ROW, None),
            P(None, every, None),
            P(None, every, None),
            P(every, None),
        ),
        check_vma=False,
    )
```

```python
import jax
import jax.numpy as jnp
from jax import lax
from jax.experimental import pallas as pl
from jax.experimental.pallas import tpu as pltpu
from jax.sharding import Mesh, PartitionSpec as P

LEAF = ("x", "z")
ROW = ("y", "core")
LEAVES = 32
ROWS = 8
HALF = 64
BLOCK = 128
F32 = jnp.float32
BF16 = jnp.bfloat16


def swap(pieces, axes):
    return lax.all_to_all(pieces, axes, split_axis=0, concat_axis=0, tiled=True)


def total(pieces):
    return jnp.sum(pieces.astype(F32), axis=0)


def copies(piece, count):
    return jnp.broadcast_to(piece[None], (count,) + piece.shape)


def leaf_terms(partial):
    return swap(partial.reshape(LEAVES, HALF, -1), LEAF)


def leaf_gather(piece):
    return swap(copies(piece.astype(BF16), LEAVES), LEAF)


def cut(array, start, size, axis):
    return lax.dynamic_slice_in_dim(array, start.astype(jnp.uint32), size, axis=axis)


def z_terms(partial):
    return swap(partial.reshape(8, HALF, -1), "z")


def z_gather(piece):
    return swap(copies(piece, 8), "z").reshape((-1,) + piece.shape[1:])


def shift(piece, axis, step):
    return lax.ppermute(piece, axis, [(i, (i + step) % 4) for i in range(4)])


def take(array, index, axis):
    return lax.dynamic_index_in_dim(array, index.astype(jnp.uint32), axis=axis, keepdims=False)


def both_cores(piece):
    return lax.all_gather(piece, "core", axis=0, tiled=False)


def row_gather(piece):
    return both_cores(swap(copies(piece, 4), "y"))


def row_half_sum(partial, core, beside=None):
    pair = total(take(both_cores(partial.reshape(2, 256, -1)), core, 1)).astype(BF16)
    others = [shift(pair, "y", step) for step in (1, 2, 3)]
    result = sum([piece.astype(F32) for piece in others], pair.astype(F32))
    return result if beside is None else (result, beside(pair))


def row_scatter(partial, core):
    halves = partial.reshape(4, 2, 256, -1)
    mine = jnp.where(core == 0, halves[:, 0], halves[:, 1])
    theirs = jnp.where(core == 0, halves[:, 1], halves[:, 0])
    pair = mine.astype(F32) + lax.ppermute(theirs, "core", [(0, 1), (1, 0)]).astype(F32)
    return total(swap(pair.astype(BF16), "y"))


def product(left, right):
    return jnp.dot(left, right, preferred_element_type=F32)


LIMITS = pltpu.CompilerParams(vmem_limit_bytes=12 * 1024 * 1024)


def forward(matrix, columns, rows_at_once=512):
    count, rows, depth = matrix.shape
    probes = columns.shape[-1]
    step = min(rows, rows_at_once)

    def kernel(matrix_ref, columns_ref, out_ref):
        out_ref[0] = product(matrix_ref[0], columns_ref[0]).astype(BF16)

    return pl.pallas_call(
        kernel,
        out_shape=jax.ShapeDtypeStruct((count, rows, probes), BF16),
        grid=(count, rows // step),
        in_specs=[
            pl.BlockSpec((1, step, depth), lambda s, m: (s, m, 0)),
            pl.BlockSpec((1, depth, probes), lambda s, m: (s, 0, 0)),
        ],
        out_specs=pl.BlockSpec((1, step, probes), lambda s, m: (s, m, 0)),
        compiler_params=LIMITS,
        name="forward",
    )(matrix, columns)


def forward_total(matrix, columns, position, landed, own_probes, carried, dtype):
    count, rows, depth = matrix.shape
    probes = columns.shape[-1]
    groups = (own_probes if carried is None else carried).shape[0]
    group = count // groups
    slots = rows // BLOCK

    def kernel(position_ref, matrix_ref, columns_ref, *refs):
        out_ref, held_ref, sems, sum_ref = refs[-4:]

        def move(member):
            return pltpu.make_async_copy(matrix_ref.at[member], held_ref.at[member], sems.at[member])

        for member in range(count):
            move(member).start()
        if carried is not None:
            sum_ref[...] = refs[0][...].astype(F32)
        else:
            landed_ref, own_ref = refs[:2]
            here, core, row = position_ref[0], position_ref[1], position_ref[2]
            own = rows // ROWS
            sum_ref[...] = jnp.zeros_like(sum_ref)
            for unit in range(groups):
                for slot in range(slots):
                    at = pl.ds(pl.multiple_of(slot * BLOCK + core * HALF, HALF), HALF)
                    sum_ref[unit, at, :] += jnp.where(here > 0, landed_ref[unit * slots + slot].astype(F32), 0.0)
                at = pl.ds(pl.multiple_of(row * own, own), own)
                sum_ref[unit, at, :] -= own_ref[unit].astype(F32)

        def step(member, carry):
            move(member).wait()
            unit = lax.div(member, group)
            sum_ref[unit] += product(held_ref[member], columns_ref[member])
            return carry

        lax.fori_loop(0, count, step, 0)
        out_ref[...] = sum_ref[...].astype(dtype)

    vmem = pl.BlockSpec(memory_space=pltpu.VMEM)
    operands = (landed, own_probes) if carried is None else (carried,)
    scratch = [
        pltpu.VMEM((count, rows, depth), BF16),
        pltpu.SemaphoreType.DMA((count,)),
        pltpu.VMEM((groups, rows, probes), F32),
    ]
    return pl.pallas_call(
        kernel,
        out_shape=jax.ShapeDtypeStruct((groups, rows, probes), dtype),
        in_specs=[pl.BlockSpec(memory_space=pltpu.SMEM), pl.BlockSpec(memory_space=pltpu.HBM), vmem]
        + [vmem] * len(operands),
        out_specs=vmem,
        scratch_shapes=scratch,
        compiler_params=LIMITS,
        name="forward_total",
    )(position, pltpu.with_memory_space_constraint(matrix, pltpu.HBM), columns, *operands)


def backward(matrix, rows_in, depth_at_once=512):
    count, depth, width = matrix.shape
    probes = rows_in.shape[-1]
    step = min(depth, depth_at_once)
    steps = depth // step

    def kernel(matrix_ref, rows_ref, out_ref, sum_ref):
        at = pl.program_id(1)

        @pl.when(at == 0)
        def _():
            sum_ref[...] = jnp.zeros_like(sum_ref)

        sum_ref[...] += product(rows_ref[0].T, matrix_ref[0])

        @pl.when(at == steps - 1)
        def _():
            out_ref[0] = sum_ref[...].T.astype(BF16)

    return pl.pallas_call(
        kernel,
        out_shape=jax.ShapeDtypeStruct((count, width, probes), BF16),
        grid=(count, steps),
        in_specs=[
            pl.BlockSpec((1, step, width), lambda s, m: (s, m, 0)),
            pl.BlockSpec((1, step, probes), lambda s, m: (s, m, 0)),
        ],
        out_specs=pl.BlockSpec((1, width, probes), lambda s, m: (s, 0, 0)),
        scratch_shapes=[pltpu.VMEM((probes, width), F32)],
        compiler_params=LIMITS,
        name="backward",
    )(matrix, rows_in)


def backward_lower(to_middle, middle_rows, to_root, root_rows):
    count, middle_depth, width = to_middle.shape
    root_depth = to_root.shape[1]
    probes = root_rows.shape[-1]

    def kernel(middle_ref, middle_rows_ref, root_ref, root_rows_ref, out_ref):
        both = product(root_rows_ref[...].T, root_ref[0]) + product(middle_rows_ref[0].T, middle_ref[0])
        out_ref[0] = both.T.astype(BF16)

    return pl.pallas_call(
        kernel,
        out_shape=jax.ShapeDtypeStruct((count, width, probes), BF16),
        grid=(count,),
        in_specs=[
            pl.BlockSpec((1, middle_depth, width), lambda s: (s, 0, 0)),
            pl.BlockSpec((1, middle_depth, probes), lambda s: (s // 2, 0, 0)),
            pl.BlockSpec((1, root_depth, width), lambda s: (s, 0, 0)),
            pl.BlockSpec((root_depth, probes), lambda s: (0, 0)),
        ],
        out_specs=pl.BlockSpec((1, width, probes), lambda s: (s, 0, 0)),
        compiler_params=LIMITS,
        name="backward_lower",
    )(to_middle, middle_rows, to_root, root_rows)


def pieces_product(matrix, held, times):
    rows, probes = matrix.shape[0], held.shape[-1]

    def kernel(matrix_ref, held_ref, out_ref):
        result = jnp.zeros((rows, probes), F32)
        for y in range(4):
            for core in range(2):
                at = (2 * y + core) * 256
                result += product(matrix_ref[:, at : at + 256], held_ref[core, y])
        rounded = result.astype(BF16)
        for copy in range(times):
            out_ref[copy] = rounded

    return pl.pallas_call(
        kernel,
        out_shape=jax.ShapeDtypeStruct((times, rows, probes), BF16),
        grid=(1,),
        in_specs=[
            pl.BlockSpec((rows, matrix.shape[1]), lambda i: (0, 0)),
            pl.BlockSpec((2, 4, 256, probes), lambda i: (0, 0, 0, 0)),
        ],
        out_specs=pl.BlockSpec((times, rows, probes), lambda i: (0, 0, 0)),
        compiler_params=LIMITS,
        name="pieces_product",
    )(matrix, held)


def body(
    leaf_probes,
    lower_probes,
    middle_probes,
    root_probes,
    leaf_inverse,
    lower_inverse,
    middle_inverse,
    root_inverse,
    leaf_panel,
    lower_to_middle,
    lower_to_root,
    middle_to_root,
    leaf_parent,
    leaf_blocks,
):
    x = lax.axis_index("x")
    z = lax.axis_index("z")
    leaf = x * 8 + z
    y = lax.axis_index("y")
    core = lax.axis_index("core")
    row = y * 2 + core
    probes = leaf_probes.shape[-1]
    inverse = leaf_inverse[0]
    panel = leaf_panel[0]

    block = take(leaf_blocks, y, 1)
    parent = leaf_parent
    slot = jnp.where(
        y < 2,
        jnp.where((parent == x) & (block % 8 == z), (x + 4 - block // 8) % 4, -1),
        jnp.where(
            y == 2,
            jnp.where(block // 2 == leaf, (parent // 2) * 2 + block % 2, -1),
            jnp.where(block // 4 == leaf, block % 4, -1),
        ),
    )
    chosen = (slot[None, :] == jnp.arange(4, dtype=jnp.int32)[:, None]).astype(F32)

    held = row_gather(leaf_probes[0])
    solved_copies = pieces_product(inverse, held, 4)
    leaf_solved = solved_copies[0]
    updates = pieces_product(panel, both_cores(swap(solved_copies, "y")), LEAVES)
    updates, tiles, pieces = lax.optimization_barrier((updates, lower_inverse, lower_probes))
    lower_held = jnp.concatenate([tiles, pieces], axis=1)
    leaving = [take(lower_held, (x + step) % 4, 0) for step in range(4)]
    lower_tiles = [leaving[0]] + [shift(leaving[step], "x", step) for step in (1, 2, 3)]
    received, lower_tiles = lax.optimization_barrier((swap(updates, LEAF), lower_tiles))
    lower_square = jnp.concatenate([tile[:512] for tile in lower_tiles], axis=1)[None]
    lower_pieces = jnp.concatenate([tile[512:] for tile in lower_tiles])
    received = received.astype(F32)
    landed = jnp.sum(chosen[:, :, None, None] * received[None], axis=1).astype(BF16)
    by_level = swap(copies(jnp.concatenate([landed.reshape(-1, probes), lower_pieces]), 4), "y")
    added = by_level[:, :256].reshape(4, 4, HALF, probes)
    lower_added = (added[0].astype(F32) + added[1].astype(F32)).astype(BF16)
    by_half = both_cores(jnp.concatenate([lower_added, by_level[:, 256:]]))
    lower_added = by_half[:, :4].transpose(1, 0, 2, 3).reshape(4, 128, probes)
    lower_own = by_half[:, 4:].reshape(2, 4, 4, 16, probes).transpose(2, 1, 0, 3, 4).reshape(4, 128, probes)
    lower_input = (lower_own.astype(F32) - lower_added.astype(F32)).astype(BF16).reshape(1, 512, probes)

    lower_terms = z_terms(forward(lower_square, lower_input))
    lower_gathered = leaf_gather(total(lower_terms))
    lower_solved = take(lower_gathered, leaf, 0)
    lower_block = lower_gathered.reshape(4, 512, probes)

    def at_level(level):
        return jnp.stack([(y == level).astype(jnp.int32), core, row])

    def early_root(pair):
        block, _ = lax.optimization_barrier((lower_block, pair))
        return forward_total(lower_to_root, block, at_level(3), landed, root_probes[None], None, BF16)

    to_middle = forward_total(lower_to_middle, lower_block, at_level(2), landed, middle_probes, None, BF16).reshape(512, probes)
    middle_half, to_root = row_half_sum(to_middle, core, early_root)
    middle_half, to_root = lax.optimization_barrier((middle_half, to_root))
    middle_input = both_cores((-middle_half).astype(BF16))

    middle_terms = leaf_terms(forward(middle_inverse, middle_input))
    middle_gathered = leaf_gather(total(middle_terms))
    middle_solved = take(middle_gathered, leaf, 0)
    middle_block = middle_gathered.reshape(2, 1024, probes)
    to_root = forward_total(middle_to_root, middle_block, at_level(3), None, None, to_root, BF16).reshape(512, probes)
    root_input = both_cores((-row_half_sum(to_root, core)).astype(BF16)).reshape(1, 512, probes)

    root_terms = leaf_terms(forward(root_inverse[None], root_input))
    root_rows = leaf_gather(total(root_terms)).reshape(1, 2048, probes)
    root_half = row_half_sum(backward(root_inverse[None], root_rows)[0], core).astype(BF16)
    root_columns = both_cores(root_half).reshape(512, probes)

    middle_drop = leaf_terms(backward(middle_to_root, jnp.broadcast_to(root_columns[None], (2, 512, probes))))
    middle_rows = leaf_gather(middle_solved.astype(F32) - total(middle_drop)).reshape(2, 1024, probes)
    middle_half = row_half_sum(backward(middle_inverse, middle_rows).reshape(512, probes), core).astype(BF16)
    middle_columns = both_cores(middle_half)

    lower_drop = backward_lower(lower_to_middle, middle_columns, lower_to_root, root_columns)
    lower_rows = z_gather((lower_solved.astype(F32) - total(leaf_terms(lower_drop))).astype(BF16))
    lower_half = row_half_sum(backward(lower_square, lower_rows[None])[0], core)
    lower_columns = both_cores(lower_half.astype(BF16)).reshape(4, 128, probes)

    stacked = jnp.where(
        y < 2,
        lower_columns.reshape(4, 2, HALF, probes),
        jnp.where(
            y == 2,
            middle_columns.reshape(4, 2, HALF, probes),
            root_columns.reshape(4, 2, HALF, probes),
        ),
    )
    table = take(stacked, core, 1)
    sent = jnp.sum(chosen[:, :, None, None] * table[:, None].astype(F32), axis=0).astype(BF16)
    ancestor = total(swap(sent, LEAF)).astype(BF16)
    leaf_back = row_scatter(backward(panel[None], ancestor[None])[0], core)
    leaf_reduced = (leaf_solved.astype(F32) - leaf_back).astype(BF16)
    leaf_solution = row_scatter(backward(inverse[None], leaf_reduced[None])[0], core).astype(BF16)

    own_rows = cut(lower_columns, row * 16, 16, 1)
    by_separator = [own_rows[0]] + [shift(own_rows[step], "x", -step) for step in (1, 2, 3)]
    lower_solution = cut(jnp.stack(by_separator + by_separator), (4 - x) % 4, 4, 0)
    middle_solution = cut(middle_columns, row * 32, 32, 1)
    root_solution = cut(root_columns, row * 64, 64, 0)
    return (leaf_solution[None], lower_solution, middle_solution, root_solution)


def solution(mesh):
    fine = Mesh(mesh.devices.reshape(4, 8, 4, 2), ("x", "z", "y", "core"))
    every = LEAF + ROW
    return jax.shard_map(
        body,
        mesh=fine,
        in_specs=(
            P(LEAF, ROW, None),
            P(None, every, None),
            P(None, every, None),
            P(every, None),
            P(LEAF, ROW, None),
            P(None, ROW, LEAF),
            P(None, ROW, LEAF),
            P(ROW, LEAF),
            P(LEAF, ROW, None),
            P(None, LEAF, ROW),
            P(None, LEAF, ROW),
            P(None, LEAF, ROW),
            P(),
            P(),
        ),
        out_specs=(
            P(LEAF, ROW, None),
            P(None, every, None),
            P(None, every, None),
            P(every, None),
        ),
        check_vma=False,
    )
```
